512 devices in a mesh: gx: 32 (over x, y, core), gy: 16 (over z).
Axes of the slice: x: 4, y: 4, z: 16, core: 2. Of those that a mesh axis runs over, the one named last changes fastest.
Arguments:
- conductance: float32 [16, 256, 2048], P(None, 'gx', 'gy'), may hold values from 0.2 to 5
- labels: int32 [16, 256, 2048], P(None, 'gx', 'gy'), may hold values from 0 to 2, as said below
- cotangent: float32 [2, 16, 256, 2048], P(None, None, 'gx', 'gy')
- saved: float32 [2, 16, 256, 2048], P(None, None, 'gx', 'gy'), may hold values from 0 to 1
Outputs:
- adjoint: float32 [2, 16, 256, 2048], P(None, None, 'gx', 'gy')
- gradient: float32 [16, 256, 2048], P(None, 'gx', 'gy')
The draws below stay inside these ranges and needn't reach their ends.
Inputs may be any that keep to these rules, and one draw needn't show every extreme that they name: `labels`: 0 marks an unseeded voxel, 1 or 2 the class of a seed.
All inputs are finite; a program needn't handle non-finite values.
Results may differ from the reference program's by a relative error of at most 0.0003.
Values sent between devices are 32-bit elements; how exact they have to be, the bound alone decides.
No kernel may reach another device: no remote copies, remote signals or barrier semaphores. Data moves between devices by JAX's collectives and lax.ppermute only.
A program may use at most 64 MiB of HBM per device.

```python
import math
import jax
import jax.numpy as jnp

Z = 16
ITERS = 3
NX = 256
NY = 2048


def draw_labels(key, part):
    picked = jax.random.randint(key, (Z, NX, NY), 0, 16)
    return jnp.where(picked == 0, 1, jnp.where(picked == 1, 2, 0)).astype(jnp.int32)


def draw_cotangent(key, part):
    key_base = jax.random.fold_in(key, 11)
    row_pos = jnp.arange(NX, dtype=jnp.float32) / float(max(NX - 1, 1))
    col_pos = jnp.arange(NY, dtype=jnp.float32) / float(max(NY - 1, 1))
    ramp = (1.0 + 2.0 * row_pos)[None, None, :, None] * (1.0 + col_pos)[None, None, None, :]
    base = jax.random.normal(key_base, (2, Z, NX, NY), jnp.float32)
    return (base * ramp * 0.5).astype(jnp.float32)


def steps_of(stream_key, dims, split, least, high):
    level = 1.0
    for dim, shards_of in split:
        draws = jax.random.uniform(jax.random.fold_in(jax.random.fold_in(stream_key, 6), dim), (shards_of,), jnp.float32, least / len(split), high / len(split))
        level = level * jnp.repeat(jnp.exp(draws), dims[dim] // shards_of).reshape((-1,) + (1,) * (len(dims) - 1 - dim))
    return level


def setup_inputs(seed: int = 0) -> dict:
    key_of = jax.random.split(jax.random.key(seed), 5)
    return {
        "conductance": jnp.clip(jnp.exp(math.log(5.0) - 3.218876 * jax.random.uniform(key_of[0], (Z, NX, NY), jnp.float32) ** steps_of(key_of[0], (Z, NX, NY), ((1, 32), (2, 16)), -0.2, 0.2)), 0.2, 5.0),
        "labels": draw_labels(jax.random.fold_in(key_of[4], 71), 0),
        "cotangent": draw_cotangent(jax.random.fold_in(key_of[4], 71), 0),
        "saved": jnp.clip(1.0 * jax.random.uniform(key_of[3], (2, Z, NX, NY), jnp.float32) ** steps_of(key_of[3], (2, Z, NX, NY), ((2, 32), (3, 16)), -0.2, 0.2), 0.0, 1.0),
    }


prior_strength = 1.0


def potentials(labels, saved):
    classes = jnp.arange(1, 3, dtype=jnp.int32)[:, None, None, None]
    tagged = labels[None]
    return jnp.where(tagged == classes, 1.0, jnp.where(tagged > 0, 0.0, saved)).astype(jnp.float32)


def edge_weights(conductance):
    edge_x = 0.5 * (conductance[:, :-1, :] + conductance[:, 1:, :])
    edge_y = 0.5 * (conductance[:, :, :-1] + conductance[:, :, 1:])
    edge_z = 0.5 * (conductance[:-1] + conductance[1:])
    return edge_x, edge_y, edge_z


def pad_after(fluxes, axis_num):
    widths = [(0, 0)] * fluxes.ndim
    widths[axis_num] = (0, 1)
    return jnp.pad(fluxes, widths)


def pad_before(fluxes, axis_num):
    widths = [(0, 0)] * fluxes.ndim
    widths[axis_num] = (1, 0)
    return jnp.pad(fluxes, widths)


def apply_graph_laplacian(input_vector, weight_field):
    edge_x, edge_y, edge_z = weight_field
    flux_x = edge_x * (-jnp.diff(input_vector, axis=2))
    flux_y = edge_y * (-jnp.diff(input_vector, axis=3))
    flux_z = edge_z * (-jnp.diff(input_vector, axis=1))
    total = pad_after(flux_x, 2) - pad_before(flux_x, 2)
    total = total + pad_after(flux_y, 3) - pad_before(flux_y, 3)
    total = total + pad_after(flux_z, 1) - pad_before(flux_z, 1)
    return total


def apply_operator(input_vector, unlabelled_mask, weight_field):
    mask_applied = unlabelled_mask * input_vector
    return unlabelled_mask * (prior_strength * mask_applied + apply_graph_laplacian(mask_applied, weight_field)) + (1.0 - unlabelled_mask) * input_vector


def edge_gradient(adjoint, potential, axis_num):
    return -jnp.sum(jnp.diff(adjoint, axis=axis_num) * jnp.diff(potential, axis=axis_num), axis=0)


def reference(conductance, labels, cotangent, saved):
    weight_field = edge_weights(conductance)
    unlabelled_mask = (labels == 0).astype(jnp.float32)[None]
    solver_residual = unlabelled_mask * cotangent
    search_direction = solver_residual
    adjoint = jnp.zeros_like(solver_residual)
    norm_now = jnp.sum(solver_residual * solver_residual, axis=(1, 2, 3))
    for iteration in range(ITERS):
        operator_result = apply_operator(search_direction, unlabelled_mask, weight_field)
        step_size = norm_now / jnp.sum(search_direction * operator_result, axis=(1, 2, 3))
        adjoint = adjoint + step_size[:, None, None, None] * search_direction
        solver_residual = solver_residual - step_size[:, None, None, None] * operator_result
        if iteration + 1 < ITERS:
            norm_next = jnp.sum(solver_residual * solver_residual, axis=(1, 2, 3))
            search_direction = solver_residual + (norm_next / norm_now)[:, None, None, None] * search_direction
            norm_now = norm_next
    potential = potentials(labels, saved)
    grad_x = edge_gradient(adjoint, potential, 2)
    grad_y = edge_gradient(adjoint, potential, 3)
    grad_z = edge_gradient(adjoint, potential, 1)
    total = pad_after(grad_x, 1) + pad_before(grad_x, 1)
    total = total + pad_after(grad_y, 2) + pad_before(grad_y, 2)
    total = total + pad_after(grad_z, 0) + pad_before(grad_z, 0)
    return adjoint, 0.5 * total
```

```python
import jax
import jax.numpy as jnp
from jax import lax
from jax.sharding import PartitionSpec as P

SHIFT = 2.0
SPAN = 32.0
ALPHA_LOW = 1.0 / 61.0


def extended(x, axis, dim, width):
    size, length = lax.axis_size(axis), x.shape[dim]
    up = [(i, i + 1) for i in range(size - 1)]
    down = [(j, i) for i, j in up]
    last = lax.slice_in_dim(x, length - width, length, axis=dim)
    first = lax.slice_in_dim(x, 0, width, axis=dim)
    before = lax.ppermute(last, axis, up)
    after = lax.ppermute(first, axis, down)
    return jnp.concatenate([before, x, after], axis=dim)


def global_sum(row):
    for axis in ("gx", "gy"):
        size = lax.axis_size(axis)
        sent = jnp.broadcast_to(row[None, None], (size, 1, row.shape[0]))
        row = jnp.sum(lax.all_to_all(sent, axis, 0, 0), axis=(0, 1))
    return row


def edge(c, dim):
    n = c.shape[dim]
    a = lax.slice_in_dim(c, 0, n - 1, axis=dim)
    b = lax.slice_in_dim(c, 1, n, axis=dim)
    return jnp.where(jnp.minimum(a, b) > 0, 0.5 * (a + b), 0.0)


def diff(v, dim):
    n = v.shape[dim]
    return lax.slice_in_dim(v, 0, n - 1, axis=dim) - lax.slice_in_dim(v, 1, n, axis=dim)


def spread(flux, dim, sign):
    low = [(0, 0)] * flux.ndim
    high = [(0, 0)] * flux.ndim
    low[dim], high[dim] = (0, 1), (1, 0)
    return jnp.pad(flux, low) + sign * jnp.pad(flux, high)


def shifted_operator(v, mask, weights):
    total = v
    for dim, w in zip((1, 2, 3), weights):
        total = total + spread(w[None] * diff(v, dim), dim, -1.0)
    return (mask * total - SHIFT * v) * (1.0 / SPAN)


def coefficients(nu):
    def inner(a, b, lift):
        total = 0.0
        for i, x in enumerate(a):
            for j, y in enumerate(b):
                total = total + (x * y) * nu[i + j + lift]
        return total

    residual = [jnp.ones_like(nu[0])]
    direction = residual
    answer = []
    norm = nu[0]
    for iteration in range(3):
        energy = SHIFT * inner(direction, direction, 0) + SPAN * inner(direction, direction, 1)
        step = jnp.clip(norm / energy, ALPHA_LOW, 1.0)
        answer = answer + [0.0]
        answer = [a + step * d for a, d in zip(answer, direction)]
        if iteration == 2:
            return answer
        image = [SHIFT * d for d in direction] + [0.0]
        image = [i + SPAN * d for i, d in zip(image, [0.0] + direction)]
        residual = [r - step * i for r, i in zip(residual + [0.0], image)]
        new = jnp.maximum(inner(residual, residual, 0), 0.0)
        ratio = new / norm
        direction = [r + ratio * d for r, d in zip(residual, direction + [0.0])]
        norm = new


def per_device(conductance, labels, cotangent, saved):
    classes = jnp.arange(1, 3, dtype=jnp.int32)[:, None, None, None]
    potential = jnp.where(labels[None] == classes, 1.0, jnp.where(labels[None] > 0, 0.0, saved))
    mask = (labels == 0).astype(jnp.float32)[None]
    fields = jnp.concatenate([conductance[None], mask, mask * cotangent, potential], axis=0)
    fields = extended(fields, "gx", 2, 3)
    fields = extended(fields, "gy", 3, 3)
    cond, mask, v0, potential = fields[0], fields[1:2], fields[2:4], fields[4:6]
    weights = [edge(cond, dim) for dim in range(3)]
    v1 = shifted_operator(v0, mask, weights)
    v2 = shifted_operator(v1, mask, weights)
    v3 = shifted_operator(v2, mask, weights)
    own = lambda v: v[:, :, 3:-3, 3:-3]
    o = [own(v) for v in (v0, v1, v2, v3)]
    moments = [jnp.sum(o[k // 2] * o[k - k // 2], axis=(1, 2, 3)) for k in range(6)]
    row = jnp.pad(jnp.concatenate(moments), (0, 116))
    row = global_sum(row)
    nu = [row[2 * k : 2 * k + 2] for k in range(6)]
    c = [x[:, None, None, None] for x in coefficients(nu)]
    adjoint = c[0] * v0 + c[1] * v1 + c[2] * v2
    adjoint = adjoint[:, :, 2:-2, 2:-2]
    potential = potential[:, :, 2:-2, 2:-2]
    valid = [(w > 0).astype(jnp.float32) for w in weights]
    gradient = 0.0
    for dim in (1, 2, 3):
        flux = jnp.sum(diff(adjoint, dim) * diff(potential, dim), axis=0)
        ok = valid[dim - 1][:, 2:-2, 2:-2]
        gradient = gradient + spread(flux * ok, dim - 1, 1.0)
    return adjoint[:, :, 1:-1, 1:-1], -0.5 * gradient[:, 1:-1, 1:-1]


def solution(mesh):
    return jax.shard_map(
        per_device,
        mesh=mesh,
        in_specs=(
            P(None, "gx", "gy"),
            P(None, "gx", "gy"),
            P(None, None, "gx", "gy"),
            P(None, None, "gx", "gy"),
        ),
        out_specs=(P(None, None, "gx", "gy"), P(None, "gx", "gy")),
        check_vma=False,
    )
```

```python
import jax
import jax.numpy as jnp
from jax import lax
from jax.experimental import pallas as pl
from jax.experimental.pallas import tpu as pltpu
from jax.sharding import PartitionSpec as P

SHIFT = 2.0
SPAN = 32.0
STEP_LOW = 1.0 / 61.0
SECOND = 64
COND, MASK, RES1, RES2, POT1, POT2 = range(6)
WIDTH = (3, 2, 3, 3, 1, 1)
LANE = (0, 9, 3, 6, 11, 12)
SLOT = (0, 6, 3, 8, 11, 12)
GROUP = 16


def roll(x, amount, axis):
    amount = amount % x.shape[axis]
    return x if amount == 0 else pltpu.roll(x, amount, axis)


def fields_at(cond, labels, cot, saved, z):
    tag = labels[z]
    free = tag == 0
    mask = jnp.where(free, 1.0, 0.0)
    pots = [jnp.where(tag == k + 1, 1.0, jnp.where(free, saved[k, z], 0.0)) for k in range(2)]
    return [cond[z], mask] + [jnp.where(free, cot[k, z], 0.0) for k in range(2)] + pots


def lanes_of(shape=(8, 128)):
    return lax.broadcasted_iota(jnp.int32, shape, 1)


def within(index, low, count):
    return (index >= low) & (index < low + count)


def pack_columns(cond, labels, cot, saved, left, right):
    lane = lanes_of()
    place = [within(lane, LANE[f], WIDTH[f]) for f in range(6)]
    depth = cond.shape[0]
    per = 128 // GROUP
    for tile in range(depth // per):
        left_tile = jnp.zeros((8, 128), jnp.float32)
        right_tile = left_tile
        for j in range(per):
            fields = fields_at(cond, labels, cot, saved, tile * per + j)
            low = jnp.zeros((8, 128), jnp.float32)
            high = low
            for f, x in enumerate(fields):
                low = jnp.where(place[f], roll(x, LANE[f], 1), low)
                high = jnp.where(place[f], roll(x, LANE[f] + WIDTH[f], 1), high)
            here = within(lane, j * GROUP, GROUP)
            left_tile = jnp.where(here, roll(low, j * GROUP, 1), left_tile)
            right_tile = jnp.where(here, roll(high, j * GROUP, 1), right_tile)
        left[tile] = left_tile
        right[tile] = right_tile


def widen(cond, labels, cot, saved, from_left, from_right, wide, top, bottom):
    lane = lanes_of()
    lane16 = lanes_of((16, 128))
    depth = cond.shape[0]
    per = 128 // GROUP
    zero = jnp.zeros((8, 128), jnp.float32)
    ends = [jnp.zeros((16, 128), jnp.float32) for _ in range(2)]
    for z in range(depth):
        fields = fields_at(cond, labels, cot, saved, z)
        tile, base = z // per, (z % per) * GROUP
        low = roll(from_left[tile], -base, 1)
        high = roll(from_right[tile], -base, 1)
        halos = []
        for f in range(6):
            w = WIDTH[f]
            before = roll(low, 128 - w - LANE[f], 1)
            after = roll(high, -LANE[f], 1)
            halos.append(jnp.where(lane < w, after, jnp.where(lane >= 128 - w, before, zero)))
        outside = (halos[COND] == 0.0) & ((lane == 0) | (lane == 127))

        def edge_value(x):
            return jnp.where(lane == 0, roll(x, 1, 1), roll(x, -1, 1))

        halos[COND] = jnp.where(outside, -edge_value(fields[COND]), halos[COND])
        for f in (POT1, POT2):
            halos[f] = jnp.where(outside, edge_value(fields[f]), halos[f])
        for f in range(6):
            wide[f, z, :, 0:128] = fields[f]
            wide[f, z, :, 128:256] = halos[f]
        for side, out in enumerate((top, bottom)):
            out[z, 13:16, :] = jnp.zeros((3, 128), jnp.float32)
            rows = []
            for f in (COND, RES1, MASK, RES2, POT1, POT2):
                w = WIDTH[f]
                start = 0 if side == 0 else 8 - w
                out[z, SLOT[f] : SLOT[f] + w, :] = fields[f][start : start + w]
                rows.append(halos[f][start : start + w])
            rows = jnp.concatenate(rows + [jnp.zeros((3, 128), jnp.float32)], axis=0)
            where = (lane16 + (128 - 8 * z + 3)) % 128 < 6
            ends[side] = jnp.where(where, roll(rows, 8 * z, 1), ends[side])
    top[depth] = ends[0]
    bottom[depth] = ends[1]


def moments(wide, from_top, from_bottom, sent, basis, pots, field, weight):
    depth = wide.shape[1]
    lane16 = lanes_of((16, 128))
    keep = (lane16 < 3) | (lane16 >= 125)
    row8 = lax.broadcasted_iota(jnp.int32, (8, 256), 0)
    for z in range(depth):
        halo = []
        for source in (from_top, from_bottom):
            end = jnp.where(keep, roll(source[depth], -8 * z, 1), 0.0)
            halo.append(jnp.concatenate([source[z], end], axis=1))
        top, bottom = halo
        parts = []
        for f in range(6):
            w, s = WIDTH[f], SLOT[f]
            own = wide[f, z]
            gap = jnp.zeros((8 - 2 * w, 256), jnp.float32)
            parts.append((own, jnp.concatenate([bottom[s : s + w], gap, top[s : s + w]], axis=0)))
        own, other = parts[COND]
        outside = (other == 0.0) & ((row8 == 0) | (row8 == 7))

        def edge_value(x):
            return jnp.where(row8 == 0, roll(x, 1, 0), roll(x, -1, 0))

        parts[COND] = (own, jnp.where(outside, -edge_value(own), other))
        for f in (POT1, POT2):
            own, other = parts[f]
            parts[f] = (own, jnp.where(outside, edge_value(own), other))
        field[0, z, 0:8], field[0, z, 8:16] = parts[COND]
        weight[3, z, 0:8] = parts[MASK][0] * (1.0 / SPAN)
        weight[3, z, 8:16] = parts[MASK][1] * (1.0 / SPAN)
        for k in range(2):
            basis[0, k, z, 0:8], basis[0, k, z, 8:16] = parts[RES1 + k]
            pots[k, z, 0:8], pots[k, z, 8:16] = parts[POT1 + k]
    for z in range(depth):
        c = field[0, z]
        weight[0, z] = 0.5 * (c + roll(c, -1, 0))
        weight[1, z] = 0.5 * (c + roll(c, -1, 1))
        if z + 1 < depth:
            weight[2, z] = 0.5 * (c + field[0, z + 1])

    def image(read, k, z, carry):
        u = read(k, z)
        fx = weight[0, z] * (u - roll(u, -1, 0))
        fy = weight[1, z] * (u - roll(u, -1, 1))
        total = (fx - roll(fx, 1, 0)) + (fy - roll(fy, 1, 1)) - u
        if carry is not None:
            total = total - carry
        carry = None
        if z + 1 < depth:
            carry = weight[2, z] * (u - read(k, z + 1))
            total = total + carry
        return weight[3, z] * total, carry

    for power in range(2):
        for k in range(2):
            carry = None
            for z in range(depth):
                value, carry = image(lambda k, z: basis[power, k, z], k, z, carry)
                basis[power + 1, k, z] = value
    totals = []
    for k in range(2):
        sums = [jnp.zeros((8, 128), jnp.float32) for _ in range(6)]
        carry = None
        for z in range(depth):
            last, carry = image(lambda k, z: basis[2, k, z], k, z, carry)
            v = [basis[i, k, z, 0:8, 0:128] for i in range(3)] + [last[0:8, 0:128]]
            sums = [s + v[i // 2] * v[i - i // 2] for i, s in enumerate(sums)]
        totals += sums
    sub = lax.broadcasted_iota(jnp.int32, (16, 128), 0)
    packed = jnp.zeros((16, 128), jnp.float32)
    for i, s in enumerate(totals):
        packed = jnp.where(sub == i, jnp.sum(s, axis=0, keepdims=True), packed)
    packed = jnp.sum(packed, axis=1, keepdims=True)
    target = jnp.where(sub < 6, sub, sub - 6 + SECOND)
    row = jnp.sum(jnp.where((lane16 == target) & (sub < 12), packed, 0.0), axis=0, keepdims=True)
    sent[...] = jnp.broadcast_to(row, sent.shape)


def relay(received, sent):
    sent[...] = jnp.broadcast_to(jnp.sum(received[...], axis=0, keepdims=True), sent.shape)


def coefficients(nu):
    def inner(a, b, lift):
        total = None
        for i, x in enumerate(a):
            for j, y in enumerate(b):
                term = (x * y) * nu[i + j + lift]
                total = term if total is None else total + term
        return total

    residual = [jnp.ones_like(nu[0])]
    direction = residual
    answer = []
    norm = nu[0]
    for iteration in range(3):
        energy = SHIFT * inner(direction, direction, 0) + SPAN * inner(direction, direction, 1)
        step = jnp.clip(norm / energy, STEP_LOW, 1.0)
        answer = [a + step * d for a, d in zip(answer + [0.0], direction)]
        if iteration == 2:
            return answer
        image = [SHIFT * d for d in direction] + [0.0]
        image = [i + SPAN * d for i, d in zip(image, [0.0] + direction)]
        residual = [r - step * i for r, i in zip(residual + [0.0], image)]
        new = jnp.maximum(inner(residual, residual, 0), 0.0)
        ratio = new / norm
        direction = [r + ratio * d for r, d in zip(residual, direction + [0.0])]
        norm = new


def finish(received, basis, pots, adjoint, gradient, field):
    depth = basis.shape[2]
    row = jnp.sum(received[...], axis=0, keepdims=True)
    row = jnp.broadcast_to(row, (8, 128))
    combined = coefficients([roll(row, -i, 1) for i in range(6)])
    lane = lanes_of()
    scale = [
        [
            jnp.sum(jnp.where(lane == k * SECOND, c, 0.0), axis=1, keepdims=True)[0:1, 0:1]
            for c in combined
        ]
        for k in range(2)
    ]
    for k in range(2):
        c = [jnp.broadcast_to(x, (16, 256)) for x in scale[k]]
        for z in range(depth):
            value = c[0] * basis[0, k, z] + c[1] * basis[1, k, z] + c[2] * basis[2, k, z]
            field[k, z] = value
            adjoint[k, z] = value[0:8, 0:128]
    carry = None
    for z in range(depth):
        gx = gy = gz = None
        for k in range(2):
            a, p = field[k, z], pots[k, z]
            tx = (a - roll(a, -1, 0)) * (p - roll(p, -1, 0))
            ty = (a - roll(a, -1, 1)) * (p - roll(p, -1, 1))
            gx = tx if gx is None else gx + tx
            gy = ty if gy is None else gy + ty
            if z + 1 < depth:
                tz = (a[0:8, 0:128] - field[k, z + 1, 0:8, 0:128]) * (
                    p[0:8, 0:128] - pots[k, z + 1, 0:8, 0:128]
                )
                gz = tz if gz is None else gz + tz
        total = (gx + roll(gx, 1, 0) + gy + roll(gy, 1, 1))[0:8, 0:128]
        if carry is not None:
            total = total + carry
        if gz is not None:
            total = total + gz
        carry = gz
        gradient[z] = -0.5 * total


def local(body, outs, scratch=()):
    vmem = pl.BlockSpec(memory_space=pltpu.VMEM)
    shapes = [jax.ShapeDtypeStruct(s, jnp.float32) for s in outs]

    def call(*args):
        return pl.pallas_call(
            body,
            out_shape=shapes,
            in_specs=[vmem] * len(args),
            out_specs=[vmem] * len(outs),
            scratch_shapes=[pltpu.VMEM(s, jnp.float32) for s in scratch],
            compiler_params=pltpu.CompilerParams(vmem_limit_bytes=32 * 1024 * 1024),
        )(*args)

    return call


def swap(low, high, axis):
    size = lax.axis_size(axis)
    up = [(i, i + 1) for i in range(size - 1)]
    down = [(j, i) for i, j in up]
    return lax.ppermute(high, axis, up), lax.ppermute(low, axis, down)


def per_device(conductance, labels, cotangent, saved):
    depth = conductance.shape[0]
    args = (conductance, labels, cotangent, saved)
    tiles = depth * GROUP // 128
    left, right = local(pack_columns, [(tiles, 8, 128)] * 2)(*args)
    from_left, from_right = swap(left, right, "gy")
    wide, top, bottom = local(widen, [(6, depth, 8, 256)] + [(depth + 1, 16, 128)] * 2)(
        *args, from_left, from_right
    )
    from_top, from_bottom = swap(top, bottom, "gx")
    rows, cols = lax.axis_size("gx"), lax.axis_size("gy")
    sent, basis, pots = local(
        moments,
        [(rows, 128), (3, 2, depth, 16, 256), (2, depth, 16, 256)],
        [(1, depth, 16, 256), (4, depth, 16, 256)],
    )(wide, from_top, from_bottom)
    received = lax.all_to_all(sent, "gx", 0, 0, tiled=True)
    (sent,) = local(relay, [(cols, 128)])(received)
    received = lax.all_to_all(sent, "gy", 0, 0, tiled=True)
    adjoint, gradient = local(finish, [cotangent.shape, conductance.shape], [(2, depth, 16, 256)])(
        received, basis, pots
    )
    return adjoint, gradient


def solution(mesh):
    return jax.shard_map(
        per_device,
        mesh=mesh,
        in_specs=(
            P(None, "gx", "gy"),
            P(None, "gx", "gy"),
            P(None, None, "gx", "gy"),
            P(None, None, "gx", "gy"),
        ),
        out_specs=(P(None, None, "gx", "gy"), P(None, "gx", "gy")),
        check_vma=False,
    )
```

```python
import jax
import jax.numpy as jnp
from jax import lax
from jax.experimental import pallas as pl
from jax.experimental.pallas import tpu as pltpu
from jax.sharding import PartitionSpec as P

SHIFT = 2.0
SPAN = 32.0
STEP_LOW = 1.0 / 61.0
SECOND = 64
COND, MASK, RES1, RES2, POT1, POT2 = range(6)
WIDTH = (3, 2, 3, 3, 1, 1)
LANE = (0, 9, 3, 6, 11, 12)
SLOT = (0, 6, 3, 8, 11, 12)
GROUP = 16


def roll(x, amount, axis):
    amount = amount % x.shape[axis]
    return x if amount == 0 else pltpu.roll(x, amount, axis)


def fields_at(cond, labels, cot, saved, z):
    tag = labels[z]
    free = tag == 0
    mask = jnp.where(free, 1.0, 0.0)
    pots = [jnp.where(tag == k + 1, 1.0, jnp.where(free, saved[k, z], 0.0)) for k in range(2)]
    return [cond[z], mask] + [jnp.where(free, cot[k, z], 0.0) for k in range(2)] + pots


def lanes_of(shape=(8, 128)):
    return lax.broadcasted_iota(jnp.int32, shape, 1)


def within(index, low, count):
    return (index >= low) & (index < low + count)


def pack_columns(cond_in, labels_in, cot_in, saved_in, first, second, field, cond, labels, cot, saved, sems):
    copies = [
        pltpu.make_async_copy(source, target, sems.at[i])
        for i, (source, target) in enumerate(
            ((cond_in, cond), (labels_in, labels), (cot_in, cot), (saved_in, saved))
        )
    ]
    for copy in copies:
        copy.start()
    for copy in copies:
        copy.wait()
    even = lax.axis_index("gy") % 2 == 0
    lane = lanes_of()
    place = [within(lane, LANE[f], WIDTH[f]) for f in range(6)]
    depth = cond.shape[0]
    per = 128 // GROUP
    for tile in range(depth // per):
        left_tile = jnp.zeros((8, 128), jnp.float32)
        right_tile = left_tile
        for j in range(per):
            z = tile * per + j
            fields = fields_at(cond, labels, cot, saved, z)
            low = jnp.zeros((8, 128), jnp.float32)
            high = low
            for f, x in enumerate(fields):
                field[f, z] = x
                low = jnp.where(place[f], roll(x, LANE[f], 1), low)
                high = jnp.where(place[f], roll(x, LANE[f] + WIDTH[f], 1), high)
            here = within(lane, j * GROUP, GROUP)
            left_tile = jnp.where(here, roll(low, j * GROUP, 1), left_tile)
            right_tile = jnp.where(here, roll(high, j * GROUP, 1), right_tile)
        first[tile] = jnp.where(even, right_tile, left_tile)
        second[tile] = jnp.where(even, left_tile, right_tile)


def widen(field, from_first, from_second, wide, near, far):
    even = lax.axis_index("gy") % 2 == 0
    upper = lax.axis_index("gx") % 2 == 0
    lane = lanes_of()
    lane16 = lanes_of((16, 128))
    depth = field.shape[1]
    per = 128 // GROUP
    zero = jnp.zeros((8, 128), jnp.float32)
    ends = [jnp.zeros((16, 128), jnp.float32) for _ in range(2)]
    for z in range(depth):
        fields = [field[f, z] for f in range(6)]
        tile, base = z // per, (z % per) * GROUP
        low = roll(jnp.where(even, from_second[tile], from_first[tile]), -base, 1)
        high = roll(jnp.where(even, from_first[tile], from_second[tile]), -base, 1)
        halos = []
        for f in range(6):
            w = WIDTH[f]
            before = roll(low, 128 - w - LANE[f], 1)
            after = roll(high, -LANE[f], 1)
            halos.append(jnp.where(lane < w, after, jnp.where(lane >= 128 - w, before, zero)))
        outside = (halos[COND] == 0.0) & ((lane == 0) | (lane == 127))

        def edge_value(x):
            return jnp.where(lane == 0, roll(x, 1, 1), roll(x, -1, 1))

        halos[COND] = jnp.where(outside, -edge_value(fields[COND]), halos[COND])
        for f in (POT1, POT2):
            halos[f] = jnp.where(outside, edge_value(fields[f]), halos[f])
        for f in range(6):
            wide[f, z, :, 0:128] = fields[f]
            wide[f, z, :, 128:256] = halos[f]
        own, end = [], []
        for side in range(2):
            rows, tips = [], []
            for f in (COND, RES1, MASK, RES2, POT1, POT2):
                w = WIDTH[f]
                start = 0 if side == 0 else 8 - w
                rows.append(fields[f][start : start + w])
                tips.append(halos[f][start : start + w])
            blank = [jnp.zeros((3, 128), jnp.float32)]
            own.append(jnp.concatenate(rows + blank, axis=0))
            end.append(jnp.concatenate(tips + blank, axis=0))
        where = (lane16 + (128 - 8 * z + 3)) % 128 < 6
        near[z] = jnp.where(upper, own[1], own[0])
        far[z] = jnp.where(upper, own[0], own[1])
        for side in range(2):
            ends[side] = jnp.where(where, roll(end[side], 8 * z, 1), ends[side])
    near[depth] = jnp.where(upper, ends[1], ends[0])
    far[depth] = jnp.where(upper, ends[0], ends[1])


def moments(wide, from_near, from_far, sent, basis, pots, field, weight):
    depth = wide.shape[1]
    core = lax.axis_index("gx") % 2
    lane16 = lanes_of((16, 128))
    keep = (lane16 < 3) | (lane16 >= 125)
    row8 = lax.broadcasted_iota(jnp.int32, (8, 256), 0)
    for z in range(depth):
        halo = []
        for source in (lambda i: from_near[1 - core, i], lambda i: from_far[i]):
            end = jnp.where(keep, roll(source(depth), -8 * z, 1), 0.0)
            halo.append(jnp.concatenate([source(z), end], axis=1))
        top = jnp.where(core == 0, halo[1], halo[0])
        bottom = jnp.where(core == 0, halo[0], halo[1])
        parts = []
        for f in range(6):
            w, s = WIDTH[f], SLOT[f]
            own = wide[f, z]
            gap = jnp.zeros((8 - 2 * w, 256), jnp.float32)
            parts.append((own, jnp.concatenate([bottom[s : s + w], gap, top[s : s + w]], axis=0)))
        own, other = parts[COND]
        outside = (other == 0.0) & ((row8 == 0) | (row8 == 7))

        def edge_value(x):
            return jnp.where(row8 == 0, roll(x, 1, 0), roll(x, -1, 0))

        parts[COND] = (own, jnp.where(outside, -edge_value(own), other))
        for f in (POT1, POT2):
            own, other = parts[f]
            parts[f] = (own, jnp.where(outside, edge_value(own), other))
        field[0, z, 0:8], field[0, z, 8:16] = parts[COND]
        weight[3, z, 0:8] = parts[MASK][0] * (1.0 / SPAN)
        weight[3, z, 8:16] = parts[MASK][1] * (1.0 / SPAN)
        for k in range(2):
            basis[0, k, z, 0:8], basis[0, k, z, 8:16] = parts[RES1 + k]
            pots[k, z, 0:8], pots[k, z, 8:16] = parts[POT1 + k]
    for z in range(depth):
        c = field[0, z]
        weight[0, z] = 0.5 * (c + roll(c, -1, 0))
        weight[1, z] = 0.5 * (c + roll(c, -1, 1))
        if z + 1 < depth:
            weight[2, z] = 0.5 * (c + field[0, z + 1])

    def image(read, k, z, carry):
        u = read(k, z)
        fx = weight[0, z] * (u - roll(u, -1, 0))
        fy = weight[1, z] * (u - roll(u, -1, 1))
        total = (fx - roll(fx, 1, 0)) + (fy - roll(fy, 1, 1)) - u
        if carry is not None:
            total = total - carry
        carry = None
        if z + 1 < depth:
            carry = weight[2, z] * (u - read(k, z + 1))
            total = total + carry
        return weight[3, z] * total, carry

    for power in range(2):
        for k in range(2):
            carry = None
            for z in range(depth):
                value, carry = image(lambda k, z: basis[power, k, z], k, z, carry)
                basis[power + 1, k, z] = value
    def own_image(k, z, carry):
        u = basis[2, k, z]
        fx = weight[0, z, :, 0:128] * (u[:, 0:128] - roll(u[:, 0:128], -1, 0))
        fx = (fx - roll(fx, 1, 0))[0:8]
        u = u[0:8]
        fy = weight[1, z, 0:8] * (u - roll(u, -1, 1))
        own = (slice(0, 8), slice(0, 128))
        total = fx + (fy - roll(fy, 1, 1))[own] - u[own]
        if carry is not None:
            total = total - carry
        carry = None
        if z + 1 < depth:
            carry = weight[2, z, 0:8, 0:128] * (u[own] - basis[2, k, z + 1, 0:8, 0:128])
            total = total + carry
        return weight[3, z, 0:8, 0:128] * total, carry

    totals = []
    for k in range(2):
        sums = [jnp.zeros((8, 128), jnp.float32) for _ in range(6)]
        carry = None
        for z in range(depth):
            last, carry = own_image(k, z, carry)
            v = [basis[i, k, z, 0:8, 0:128] for i in range(3)] + [last]
            sums = [s + v[i // 2] * v[i - i // 2] for i, s in enumerate(sums)]
        totals += sums
    sub = lax.broadcasted_iota(jnp.int32, (16, 128), 0)
    packed = jnp.zeros((16, 128), jnp.float32)
    for i, s in enumerate(totals):
        packed = jnp.where(sub == i, jnp.sum(s, axis=0, keepdims=True), packed)
    packed = jnp.sum(packed, axis=1, keepdims=True)
    target = jnp.where(sub < 6, sub, sub - 6 + SECOND)
    row = jnp.sum(jnp.where((lane16 == target) & (sub < 12), packed, 0.0), axis=0, keepdims=True)
    sent[...] = jnp.broadcast_to(row, sent.shape)


def relay(received, sent):
    sent[...] = jnp.broadcast_to(jnp.sum(received[...], axis=0, keepdims=True), sent.shape)


def coefficients(nu):
    def inner(a, b, lift):
        total = None
        for i, x in enumerate(a):
            for j, y in enumerate(b):
                term = (x * y) * nu[i + j + lift]
                total = term if total is None else total + term
        return total

    residual = [jnp.ones_like(nu[0])]
    direction = residual
    answer = []
    norm = nu[0]
    for iteration in range(3):
        energy = SHIFT * inner(direction, direction, 0) + SPAN * inner(direction, direction, 1)
        step = jnp.clip(norm / energy, STEP_LOW, 1.0)
        answer = [a + step * d for a, d in zip(answer + [0.0], direction)]
        if iteration == 2:
            return answer
        image = [SHIFT * d for d in direction] + [0.0]
        image = [i + SPAN * d for i, d in zip(image, [0.0] + direction)]
        residual = [r - step * i for r, i in zip(residual + [0.0], image)]
        new = jnp.maximum(inner(residual, residual, 0), 0.0)
        ratio = new / norm
        direction = [r + ratio * d for r, d in zip(residual, direction + [0.0])]
        norm = new


def finish(received, basis, pots, adjoint, gradient, field):
    depth = basis.shape[2]
    row = jnp.sum(received[...], axis=0, keepdims=True)
    row = jnp.broadcast_to(row, (8, 128))
    combined = coefficients([roll(row, -i, 1) for i in range(6)])
    lane = lanes_of()
    scale = [
        [
            jnp.sum(jnp.where(lane == k * SECOND, c, 0.0), axis=1, keepdims=True)[0:1, 0:1]
            for c in combined
        ]
        for k in range(2)
    ]
    for k in range(2):
        c = [jnp.broadcast_to(x, (16, 256)) for x in scale[k]]
        for z in range(depth):
            value = c[0] * basis[0, k, z] + c[1] * basis[1, k, z] + c[2] * basis[2, k, z]
            field[k, z] = value
            adjoint[k, z] = value[0:8, 0:128]
    carry = None
    for z in range(depth):
        gx = gy = gz = None
        for k in range(2):
            a, p = field[k, z], pots[k, z]
            tx = (a - roll(a, -1, 0)) * (p - roll(p, -1, 0))
            ty = (a - roll(a, -1, 1)) * (p - roll(p, -1, 1))
            gx = tx if gx is None else gx + tx
            gy = ty if gy is None else gy + ty
            if z + 1 < depth:
                tz = (a[0:8, 0:128] - field[k, z + 1, 0:8, 0:128]) * (
                    p[0:8, 0:128] - pots[k, z + 1, 0:8, 0:128]
                )
                gz = tz if gz is None else gz + tz
        total = (gx + roll(gx, 1, 0) + gy + roll(gy, 1, 1))[0:8, 0:128]
        if carry is not None:
            total = total + carry
        if gz is not None:
            total = total + gz
        carry = gz
        gradient[z] = -0.5 * total


def local(body, outs, scratch=(), space=pltpu.VMEM, limit=32 * 2**20, kind=pltpu.VMEM):
    vmem = pl.BlockSpec(memory_space=pltpu.VMEM)
    shapes = [kind(s, jnp.float32) for s in outs]

    def call(*args):
        return pl.pallas_call(
            body,
            out_shape=shapes,
            in_specs=[pl.BlockSpec(memory_space=space)] * len(args),
            out_specs=[vmem] * len(outs),
            scratch_shapes=list(scratch),
            compiler_params=pltpu.CompilerParams(vmem_limit_bytes=limit),
        )(*args)

    return call


def scratch(*shape, dtype=jnp.float32):
    return pltpu.VMEM(shape, dtype)


def trade(x, axis, start):
    pairs = [(i, i + 1) for i in range(start, lax.axis_size(axis) - 1, 2)]
    return lax.ppermute(x, axis, pairs + [(j, i) for i, j in pairs])


def per_device(conductance, labels, cotangent, saved):
    depth = conductance.shape[0]
    rows, cols = lax.axis_size("gx"), lax.axis_size("gy")
    args = (conductance, labels, cotangent, saved)
    tiles = depth * GROUP // 128
    first, second, field = local(
        pack_columns,
        [(tiles, 8, 128)] * 2 + [(6, depth, 8, 128)],
        [scratch(*x.shape, dtype=x.dtype) for x in args] + [pltpu.SemaphoreType.DMA((4,))],
        pltpu.HBM,
        56 * 2**20,
    )(*args)
    first, second = trade(first, "gy", 0), trade(second, "gy", 1)
    wide, near, far = local(widen, [(6, depth, 8, 256)] + [(depth + 1, 16, 128)] * 2)(
        field, first, second
    )
    far = trade(far, "gx", 1)
    near = lax.all_gather(near, "gx", axis_index_groups=[[i, i + 1] for i in range(0, rows, 2)])
    sent, basis, pots = local(
        moments,
        [(rows, 128), (3, 2, depth, 16, 256), (2, depth, 16, 256)],
        [scratch(1, depth, 16, 256), scratch(4, depth, 16, 256)],
    )(wide, near, far)
    received = lax.all_to_all(sent, "gx", 0, 0, tiled=True)
    (sent,) = local(relay, [(cols, 128)])(received)
    received = lax.all_to_all(sent, "gy", 0, 0, tiled=True)
    adjoint, gradient = local(
        finish, [cotangent.shape, conductance.shape], [scratch(2, depth, 16, 256)],
        kind=jax.ShapeDtypeStruct,
    )(received, basis, pots)
    return adjoint, gradient


def solution(mesh):
    return jax.shard_map(
        per_device,
        mesh=mesh,
        in_specs=(
            P(None, "gx", "gy"),
            P(None, "gx", "gy"),
            P(None, None, "gx", "gy"),
            P(None, None, "gx", "gy"),
        ),
        out_specs=(P(None, None, "gx", "gy"), P(None, "gx", "gy")),
        check_vma=False,
    )
```

```python
import jax
import jax.numpy as jnp
from jax import lax
from jax.experimental import pallas as pl
from jax.experimental.pallas import tpu as pltpu
from jax.sharding import PartitionSpec as P

SHIFT = 2.0
SPAN = 32.0
STEP_LOW = 1.0 / 61.0
SECOND = 64
COND, MASK, RES1, RES2, POT1, POT2 = range(6)
WIDTH = (3, 2, 3, 3, 1, 1)
LANE = (0, 9, 3, 6, 11, 12)
SLOT = (0, 6, 3, 8, 11, 12)
GROUP = 16


def roll(x, amount, axis):
    amount = amount % x.shape[axis]
    return x if amount == 0 else pltpu.roll(x, amount, axis)


def fields_at(cond, labels, cot, saved, z):
    tag = labels[z]
    free = tag == 0
    mask = jnp.where(free, 1.0, 0.0)
    pots = [jnp.where(tag == k + 1, 1.0, jnp.where(free, saved[k, z], 0.0)) for k in range(2)]
    return [cond[z], mask] + [jnp.where(free, cot[k, z], 0.0) for k in range(2)] + pots


def lanes_of(shape=(8, 128)):
    return lax.broadcasted_iota(jnp.int32, shape, 1)


def within(index, low, count):
    return (index >= low) & (index < low + count)


def pack_columns(cond_in, labels_in, cot_in, saved_in, first, second, field, cond, labels, cot, saved, sems):
    copies = [
        pltpu.make_async_copy(source, target, sems.at[i])
        for i, (source, target) in enumerate(
            ((cond_in, cond), (labels_in, labels), (cot_in, cot), (saved_in, saved))
        )
    ]
    for copy in copies:
        copy.start()
    for copy in copies:
        copy.wait()
    even = lax.axis_index("gy") % 2 == 0
    lane = lanes_of()
    place = [within(lane, LANE[f], WIDTH[f]) for f in range(6)]
    depth = cond.shape[0]
    per = 128 // GROUP
    for tile in range(depth // per):
        left_tile = jnp.zeros((8, 128), jnp.float32)
        right_tile = left_tile
        for j in range(per):
            z = tile * per + j
            fields = fields_at(cond, labels, cot, saved, z)
            low = jnp.zeros((8, 128), jnp.float32)
            high = low
            for f, x in enumerate(fields):
                field[f, z] = x
                low = jnp.where(place[f], roll(x, LANE[f], 1), low)
                high = jnp.where(place[f], roll(x, LANE[f] + WIDTH[f], 1), high)
            here = within(lane, j * GROUP, GROUP)
            left_tile = jnp.where(here, roll(low, j * GROUP, 1), left_tile)
            right_tile = jnp.where(here, roll(high, j * GROUP, 1), right_tile)
        first[tile] = jnp.where(even, right_tile, left_tile)
        second[tile] = jnp.where(even, left_tile, right_tile)


def widen(field, from_first, from_second, wide, near, far):
    even = lax.axis_index("gy") % 2 == 0
    upper = lax.axis_index("gx") % 2 == 0
    lane = lanes_of()
    lane16 = lanes_of((16, 128))
    depth = field.shape[1]
    per = 128 // GROUP
    zero = jnp.zeros((8, 128), jnp.float32)
    ends = [jnp.zeros((16, 128), jnp.float32) for _ in range(2)]
    for z in range(depth):
        fields = [field[f, z] for f in range(6)]
        tile, base = z // per, (z % per) * GROUP
        low = roll(jnp.where(even, from_second[tile], from_first[tile]), -base, 1)
        high = roll(jnp.where(even, from_first[tile], from_second[tile]), -base, 1)
        halos = []
        for f in range(6):
            w = WIDTH[f]
            before = roll(low, 128 - w - LANE[f], 1)
            after = roll(high, -LANE[f], 1)
            halos.append(jnp.where(lane < w, after, jnp.where(lane >= 128 - w, before, zero)))
        outside = (halos[COND] == 0.0) & ((lane == 0) | (lane == 127))

        def edge_value(x):
            return jnp.where(lane == 0, roll(x, 1, 1), roll(x, -1, 1))

        halos[COND] = jnp.where(outside, -edge_value(fields[COND]), halos[COND])
        for f in (POT1, POT2):
            halos[f] = jnp.where(outside, edge_value(fields[f]), halos[f])
        for f in range(6):
            wide[f, z, :, 0:128] = fields[f]
            wide[f, z, :, 128:256] = halos[f]
        own, end = [], []
        for side in range(2):
            rows, tips = [], []
            for f in (COND, RES1, MASK, RES2, POT1, POT2):
                w = WIDTH[f]
                start = 0 if side == 0 else 8 - w
                rows.append(fields[f][start : start + w])
                tips.append(halos[f][start : start + w])
            blank = [jnp.zeros((3, 128), jnp.float32)]
            own.append(jnp.concatenate(rows + blank, axis=0))
            end.append(jnp.concatenate(tips + blank, axis=0))
        where = (lane16 + (128 - 8 * z + 3)) % 128 < 6
        near[z] = jnp.where(upper, own[1], own[0])
        far[z] = jnp.where(upper, own[0], own[1])
        for side in range(2):
            ends[side] = jnp.where(where, roll(end[side], 8 * z, 1), ends[side])
    near[depth] = jnp.where(upper, ends[1], ends[0])
    far[depth] = jnp.where(upper, ends[0], ends[1])


def moments(wide, from_near, from_far, sent, basis, pots, field, weight):
    depth = wide.shape[1]
    core = lax.axis_index("gx") % 2
    lane16 = lanes_of((16, 128))
    keep = (lane16 < 3) | (lane16 >= 125)
    row8 = lax.broadcasted_iota(jnp.int32, (8, 256), 0)
    for z in range(depth):
        halo = []
        for source in (lambda i: from_near[1 - core, i], lambda i: from_far[i]):
            end = jnp.where(keep, roll(source(depth), -8 * z, 1), 0.0)
            halo.append(jnp.concatenate([source(z), end], axis=1))
        top = jnp.where(core == 0, halo[1], halo[0])
        bottom = jnp.where(core == 0, halo[0], halo[1])
        parts = []
        for f in range(6):
            w, s = WIDTH[f], SLOT[f]
            own = wide[f, z]
            gap = jnp.zeros((8 - 2 * w, 256), jnp.float32)
            parts.append((own, jnp.concatenate([bottom[s : s + w], gap, top[s : s + w]], axis=0)))
        own, other = parts[COND]
        outside = (other == 0.0) & ((row8 == 0) | (row8 == 7))

        def edge_value(x):
            return jnp.where(row8 == 0, roll(x, 1, 0), roll(x, -1, 0))

        parts[COND] = (own, jnp.where(outside, -edge_value(own), other))
        for f in (POT1, POT2):
            own, other = parts[f]
            parts[f] = (own, jnp.where(outside, edge_value(own), other))
        field[0, z, 0:8], field[0, z, 8:16] = parts[COND]
        weight[3, z, 0:8] = parts[MASK][0] * (1.0 / SPAN)
        weight[3, z, 8:16] = parts[MASK][1] * (1.0 / SPAN)
        for k in range(2):
            basis[0, k, z, 0:8], basis[0, k, z, 8:16] = parts[RES1 + k]
            pots[k, z, 0:8], pots[k, z, 8:16] = parts[POT1 + k]
    for z in range(depth):
        c = field[0, z]
        weight[0, z] = 0.5 * (c + roll(c, -1, 0))
        weight[1, z] = 0.5 * (c + roll(c, -1, 1))
        if z + 1 < depth:
            weight[2, z] = 0.5 * (c + field[0, z + 1])

    def image(read, k, z, carry):
        u = read(k, z)
        fx = weight[0, z] * (u - roll(u, -1, 0))
        fy = weight[1, z] * (u - roll(u, -1, 1))
        total = (fx - roll(fx, 1, 0)) + (fy - roll(fy, 1, 1)) - u
        if carry is not None:
            total = total - carry
        carry = None
        if z + 1 < depth:
            carry = weight[2, z] * (u - read(k, z + 1))
            total = total + carry
        return weight[3, z] * total, carry

    for power in range(2):
        for k in range(2):
            carry = None
            for z in range(depth):
                value, carry = image(lambda k, z: basis[power, k, z], k, z, carry)
                basis[power + 1, k, z] = value
    def own_image(k, z, carry):
        u = basis[2, k, z]
        fx = weight[0, z, :, 0:128] * (u[:, 0:128] - roll(u[:, 0:128], -1, 0))
        fx = (fx - roll(fx, 1, 0))[0:8]
        u = u[0:8]
        fy = weight[1, z, 0:8] * (u - roll(u, -1, 1))
        own = (slice(0, 8), slice(0, 128))
        total = fx + (fy - roll(fy, 1, 1))[own] - u[own]
        if carry is not None:
            total = total - carry
        carry = None
        if z + 1 < depth:
            carry = weight[2, z, 0:8, 0:128] * (u[own] - basis[2, k, z + 1, 0:8, 0:128])
            total = total + carry
        return weight[3, z, 0:8, 0:128] * total, carry

    totals = []
    for k in range(2):
        sums = [jnp.zeros((8, 128), jnp.float32) for _ in range(6)]
        carry = None
        for z in range(depth):
            last, carry = own_image(k, z, carry)
            v = [basis[i, k, z, 0:8, 0:128] for i in range(3)] + [last]
            sums = [s + v[i // 2] * v[i - i // 2] for i, s in enumerate(sums)]
        totals += sums
    sub = lax.broadcasted_iota(jnp.int32, (16, 128), 0)
    packed = jnp.zeros((16, 128), jnp.float32)
    for i, s in enumerate(totals):
        packed = jnp.where(sub == i, jnp.sum(s, axis=0, keepdims=True), packed)
    packed = jnp.sum(packed, axis=1, keepdims=True)
    target = jnp.where(sub < 6, sub, sub - 6 + SECOND)
    row = jnp.sum(jnp.where((lane16 == target) & (sub < 12), packed, 0.0), axis=0, keepdims=True)
    sent[...] = jnp.broadcast_to(row, sent.shape)


def relay(received, sent):
    sent[...] = jnp.broadcast_to(jnp.sum(received[...], axis=0, keepdims=True), sent.shape)


def coefficients(nu):
    def inner(a, b, lift):
        total = None
        for i, x in enumerate(a):
            for j, y in enumerate(b):
                term = (x * y) * nu[i + j + lift]
                total = term if total is None else total + term
        return total

    residual = [jnp.ones_like(nu[0])]
    direction = residual
    answer = []
    norm = nu[0]
    for iteration in range(3):
        energy = SHIFT * inner(direction, direction, 0) + SPAN * inner(direction, direction, 1)
        step = jnp.clip(norm / energy, STEP_LOW, 1.0)
        answer = [a + step * d for a, d in zip(answer + [0.0], direction)]
        if iteration == 2:
            return answer
        image = [SHIFT * d for d in direction] + [0.0]
        image = [i + SPAN * d for i, d in zip(image, [0.0] + direction)]
        residual = [r - step * i for r, i in zip(residual + [0.0], image)]
        new = jnp.maximum(inner(residual, residual, 0), 0.0)
        ratio = new / norm
        direction = [r + ratio * d for r, d in zip(residual, direction + [0.0])]
        norm = new


def finish(received, basis, pots, adjoint, gradient, field):
    depth = basis.shape[2]
    row = jnp.sum(received[...], axis=0, keepdims=True)
    row = jnp.broadcast_to(row, (8, 128))
    combined = coefficients([roll(row, -i, 1) for i in range(6)])
    lane = lanes_of()
    scale = [
        [
            jnp.sum(jnp.where(lane == k * SECOND, c, 0.0), axis=1, keepdims=True)[0:1, 0:1]
            for c in combined
        ]
        for k in range(2)
    ]
    for k in range(2):
        c = [jnp.broadcast_to(x, (16, 256)) for x in scale[k]]
        for z in range(depth):
            value = c[0] * basis[0, k, z] + c[1] * basis[1, k, z] + c[2] * basis[2, k, z]
            field[k, z] = value
            adjoint[k, z] = value[0:8, 0:128]
    carry = None
    for z in range(depth):
        gx = gy = gz = None
        for k in range(2):
            a, p = field[k, z], pots[k, z]
            tx = (a - roll(a, -1, 0)) * (p - roll(p, -1, 0))
            ty = (a - roll(a, -1, 1)) * (p - roll(p, -1, 1))
            gx = tx if gx is None else gx + tx
            gy = ty if gy is None else gy + ty
            if z + 1 < depth:
                tz = (a[0:8, 0:128] - field[k, z + 1, 0:8, 0:128]) * (
                    p[0:8, 0:128] - pots[k, z + 1, 0:8, 0:128]
                )
                gz = tz if gz is None else gz + tz
        total = (gx + roll(gx, 1, 0) + gy + roll(gy, 1, 1))[0:8, 0:128]
        if carry is not None:
            total = total + carry
        if gz is not None:
            total = total + gz
        carry = gz
        gradient[z] = -0.5 * total


def local(body, outs, scratch=(), space=pltpu.VMEM, limit=32 * 2**20, kind=pltpu.VMEM):
    vmem = pl.BlockSpec(memory_space=pltpu.VMEM)
    shapes = [kind(s, jnp.float32) for s in outs]

    def call(*args):
        return pl.pallas_call(
            body,
            out_shape=shapes,
            in_specs=[pl.BlockSpec(memory_space=space)] * len(args),
            out_specs=[vmem] * len(outs),
            scratch_shapes=list(scratch),
            compiler_params=pltpu.CompilerParams(vmem_limit_bytes=limit),
        )(*args)

    return call


def scratch(*shape, dtype=jnp.float32):
    return pltpu.VMEM(shape, dtype)


def trade(x, axis, start):
    pairs = [(i, i + 1) for i in range(start, lax.axis_size(axis) - 1, 2)]
    return lax.ppermute(x, axis, pairs + [(j, i) for i, j in pairs])


def per_device(conductance, labels, cotangent, saved):
    depth = conductance.shape[0]
    rows, cols = lax.axis_size("gx"), lax.axis_size("gy")
    args = (conductance, labels, cotangent, saved)
    tiles = depth * GROUP // 128
    first, second, field = local(
        pack_columns,
        [(tiles, 8, 128)] * 2 + [(6, depth, 8, 128)],
        [scratch(*x.shape, dtype=x.dtype) for x in args] + [pltpu.SemaphoreType.DMA((4,))],
        pltpu.HBM,
        56 * 2**20,
    )(*args)
    first, second = trade(first, "gy", 0), trade(second, "gy", 1)
    wide, near, far = local(widen, [(6, depth, 8, 256)] + [(depth + 1, 16, 128)] * 2)(
        field, first, second
    )
    far = trade(far, "gx", 1)
    near = lax.all_gather(near, "gx", axis_index_groups=[[i, i + 1] for i in range(0, rows, 2)])
    sent, basis, pots = local(
        moments,
        [(cols, 128), (3, 2, depth, 16, 256), (2, depth, 16, 256)],
        [scratch(1, depth, 16, 256), scratch(4, depth, 16, 256)],
    )(wide, near, far)
    received = lax.all_to_all(sent, "gy", 0, 0, tiled=True)
    (sent,) = local(relay, [(rows, 128)])(received)
    received = lax.all_to_all(sent, "gx", 0, 0, tiled=True)
    adjoint, gradient = local(
        finish, [cotangent.shape, conductance.shape], [scratch(2, depth, 16, 256)],
        kind=jax.ShapeDtypeStruct,
    )(received, basis, pots)
    return adjoint, gradient


def solution(mesh):
    return jax.shard_map(
        per_device,
        mesh=mesh,
        in_specs=(
            P(None, "gx", "gy"),
            P(None, "gx", "gy"),
            P(None, None, "gx", "gy"),
            P(None, None, "gx", "gy"),
        ),
        out_specs=(P(None, None, "gx", "gy"), P(None, "gx", "gy")),
        check_vma=False,
    )
```

```python
import jax
import jax.numpy as jnp
from jax import lax
from jax.experimental import pallas as pl
from jax.experimental.pallas import tpu as pltpu
from jax.sharding import PartitionSpec as P

SHIFT = 2.0
SPAN = 32.0
STEP_LOW = 1.0 / 61.0
SECOND = 64
COND, MASK, RES1, RES2, POT1, POT2 = range(6)
WIDTH = (3, 2, 3, 3, 1, 1)
LANE = (0, 9, 3, 6, 11, 12)
SLOT = (0, 6, 3, 8, 11, 12)
GROUP = 16


def roll(x, amount, axis):
    amount = amount % x.shape[axis]
    return x if amount == 0 else pltpu.roll(x, amount, axis)


def fields_at(cond, labels, cot, saved, z):
    tag = labels[z]
    free = tag == 0
    mask = jnp.where(free, 1.0, 0.0)
    pots = [jnp.where(tag == k + 1, 1.0, jnp.where(free, saved[k, z], 0.0)) for k in range(2)]
    return [cond[z], mask] + [jnp.where(free, cot[k, z], 0.0) for k in range(2)] + pots


def lanes_of(shape=(8, 128)):
    return lax.broadcasted_iota(jnp.int32, shape, 1)


def within(index, low, count):
    return (index >= low) & (index < low + count)


def pack_columns(cond_in, labels_in, cot_in, saved_in, first, second, field, cond, labels, cot, saved, sems):
    copies = [
        pltpu.make_async_copy(source, target, sems.at[i])
        for i, (source, target) in enumerate(
            ((cond_in, cond), (labels_in, labels), (cot_in, cot), (saved_in, saved))
        )
    ]
    for copy in copies:
        copy.start()
    for copy in copies:
        copy.wait()
    even = lax.axis_index("gy") % 2 == 0
    lane = lanes_of()
    place = [within(lane, LANE[f], WIDTH[f]) for f in range(6)]
    depth = cond.shape[0]
    per = 128 // GROUP
    for tile in range(depth // per):
        left_tile = jnp.zeros((8, 128), jnp.float32)
        right_tile = left_tile
        for j in range(per):
            z = tile * per + j
            fields = fields_at(cond, labels, cot, saved, z)
            low = jnp.zeros((8, 128), jnp.float32)
            high = low
            for f, x in enumerate(fields):
                field[f, z] = x
                low = jnp.where(place[f], roll(x, LANE[f], 1), low)
                high = jnp.where(place[f], roll(x, LANE[f] + WIDTH[f], 1), high)
            here = within(lane, j * GROUP, GROUP)
            left_tile = jnp.where(here, roll(low, j * GROUP, 1), left_tile)
            right_tile = jnp.where(here, roll(high, j * GROUP, 1), right_tile)
        first[tile] = jnp.where(even, right_tile, left_tile)
        second[tile] = jnp.where(even, left_tile, right_tile)


def widen(field, from_first, from_second, wide, near, far):
    even = lax.axis_index("gy") % 2 == 0
    upper = lax.axis_index("gx") % 2 == 0
    lane = lanes_of()
    lane16 = lanes_of((16, 128))
    depth = field.shape[1]
    per = 128 // GROUP
    zero = jnp.zeros((8, 128), jnp.float32)
    ends = [jnp.zeros((16, 128), jnp.float32) for _ in range(2)]
    for z in range(depth):
        fields = [field[f, z] for f in range(6)]
        tile, base = z // per, (z % per) * GROUP
        low = roll(jnp.where(even, from_second[tile], from_first[tile]), -base, 1)
        high = roll(jnp.where(even, from_first[tile], from_second[tile]), -base, 1)
        halos = []
        for f in range(6):
            w = WIDTH[f]
            before = roll(low, 128 - w - LANE[f], 1)
            after = roll(high, -LANE[f], 1)
            halos.append(jnp.where(lane < w, after, jnp.where(lane >= 128 - w, before, zero)))
        outside = (halos[COND] == 0.0) & ((lane == 0) | (lane == 127))

        def edge_value(x):
            return jnp.where(lane == 0, roll(x, 1, 1), roll(x, -1, 1))

        halos[COND] = jnp.where(outside, -edge_value(fields[COND]), halos[COND])
        for f in (POT1, POT2):
            halos[f] = jnp.where(outside, edge_value(fields[f]), halos[f])
        for f in range(6):
            wide[f, z, :, 0:128] = fields[f]
            wide[f, z, :, 128:256] = halos[f]
        own, end = [], []
        for side in range(2):
            rows, tips = [], []
            for f in (COND, RES1, MASK, RES2, POT1, POT2):
                w = WIDTH[f]
                start = 0 if side == 0 else 8 - w
                rows.append(fields[f][start : start + w])
                tips.append(halos[f][start : start + w])
            blank = [jnp.zeros((3, 128), jnp.float32)]
            own.append(jnp.concatenate(rows + blank, axis=0))
            end.append(jnp.concatenate(tips + blank, axis=0))
        where = (lane16 + (128 - 8 * z + 3)) % 128 < 6
        near[z] = jnp.where(upper, own[1], own[0])
        far[z] = jnp.where(upper, own[0], own[1])
        for side in range(2):
            ends[side] = jnp.where(where, roll(end[side], 8 * z, 1), ends[side])
    near[depth] = jnp.where(upper, ends[1], ends[0])
    far[depth] = jnp.where(upper, ends[0], ends[1])


def exact_dot(x, matrix):
    total = None
    for _ in range(3):
        term = x.astype(jnp.bfloat16)
        x = x - term.astype(jnp.float32)
        part = jnp.dot(term, matrix, preferred_element_type=jnp.float32)
        total = part if total is None else total + part
    return total


def difference_matrices():
    i = lax.broadcasted_iota(jnp.int32, (256, 256), 0)
    j = lax.broadcasted_iota(jnp.int32, (256, 256), 1)
    here = jnp.where(i == j, 1.0, 0.0)
    forward = here - jnp.where(i == (j + 1) % 256, 1.0, 0.0)
    backward = here - jnp.where((i + 1) % 256 == j, 1.0, 0.0)
    return forward.astype(jnp.bfloat16), backward.astype(jnp.bfloat16)


def moments(wide, from_near, from_far, sent, basis, pots, field, weight, flux):
    depth = wide.shape[1]
    core = lax.axis_index("gx") % 2
    lane16 = lanes_of((16, 128))
    keep = (lane16 < 3) | (lane16 >= 125)
    row8 = lax.broadcasted_iota(jnp.int32, (8, 256), 0)
    for z in range(depth):
        halo = []
        for source in (lambda i: from_near[1 - core, i], lambda i: from_far[i]):
            end = jnp.where(keep, roll(source(depth), -8 * z, 1), 0.0)
            halo.append(jnp.concatenate([source(z), end], axis=1))
        top = jnp.where(core == 0, halo[1], halo[0])
        bottom = jnp.where(core == 0, halo[0], halo[1])
        parts = []
        for f in range(6):
            w, s = WIDTH[f], SLOT[f]
            own = wide[f, z]
            gap = jnp.zeros((8 - 2 * w, 256), jnp.float32)
            parts.append((own, jnp.concatenate([bottom[s : s + w], gap, top[s : s + w]], axis=0)))
        own, other = parts[COND]
        outside = (other == 0.0) & ((row8 == 0) | (row8 == 7))

        def edge_value(x):
            return jnp.where(row8 == 0, roll(x, 1, 0), roll(x, -1, 0))

        parts[COND] = (own, jnp.where(outside, -edge_value(own), other))
        for f in (POT1, POT2):
            own, other = parts[f]
            parts[f] = (own, jnp.where(outside, edge_value(own), other))
        field[0, z, 0:8], field[0, z, 8:16] = parts[COND]
        weight[3, z, 0:8] = parts[MASK][0] * (1.0 / SPAN)
        weight[3, z, 8:16] = parts[MASK][1] * (1.0 / SPAN)
        for k in range(2):
            basis[0, k, z, 0:8], basis[0, k, z, 8:16] = parts[RES1 + k]
            pots[k, z, 0:8], pots[k, z, 8:16] = parts[POT1 + k]
    for z in range(depth):
        c = field[0, z]
        weight[0, z] = 0.5 * (c + roll(c, -1, 0))
        weight[1, z] = 0.5 * (c + roll(c, -1, 1))
        if z + 1 < depth:
            weight[2, z] = 0.5 * (c + field[0, z + 1])

    forward, backward = difference_matrices()

    def image(k, z, source, carry):
        u = basis[source, k, z]
        fx = weight[0, z] * (u - roll(u, -1, 0))
        total = (fx - roll(fx, 1, 0)) + flux[k, z] - u
        if carry is not None:
            total = total - carry
        carry = None
        if z + 1 < depth:
            carry = weight[2, z] * (u - basis[source, k, z + 1])
            total = total + carry
        return weight[3, z] * total, carry

    def lane_fluxes(source, rows):
        for k in range(2):
            u = basis[source, k, :, 0:rows].reshape(depth * rows, 256)
            f = weight[1, :, 0:rows].reshape(depth * rows, 256) * exact_dot(u, forward)
            flux[k, :, 0:rows] = exact_dot(f, backward).reshape(depth, rows, 256)

    for power in range(2):
        lane_fluxes(power, 16)
        for k in range(2):
            carry = None
            for z in range(depth):
                value, carry = image(k, z, power, carry)
                basis[power + 1, k, z] = value
    own = (slice(0, 8), slice(0, 128))

    def own_image(k, z, carry):
        u = basis[2, k, z, :, 0:128]
        fx = weight[0, z, :, 0:128] * (u - roll(u, -1, 0))
        u = u[0:8]
        total = (fx - roll(fx, 1, 0))[0:8] + flux[k, z, 0:8, 0:128] - u
        if carry is not None:
            total = total - carry
        carry = None
        if z + 1 < depth:
            carry = weight[2, z, 0:8, 0:128] * (u - basis[2, k, z + 1, 0:8, 0:128])
            total = total + carry
        return weight[3, z, 0:8, 0:128] * total, carry

    lane_fluxes(2, 8)
    totals = []
    for k in range(2):
        sums = [jnp.zeros((8, 128), jnp.float32) for _ in range(6)]
        carry = None
        for z in range(depth):
            last, carry = own_image(k, z, carry)
            v = [basis[i, k, z, 0:8, 0:128] for i in range(3)] + [last]
            sums = [s + v[i // 2] * v[i - i // 2] for i, s in enumerate(sums)]
        totals += sums
    sub = lax.broadcasted_iota(jnp.int32, (16, 128), 0)
    packed = jnp.zeros((16, 128), jnp.float32)
    for i, s in enumerate(totals):
        packed = jnp.where(sub == i, jnp.sum(s, axis=0, keepdims=True), packed)
    packed = jnp.sum(packed, axis=1, keepdims=True)
    target = jnp.where(sub < 6, sub, sub - 6 + SECOND)
    row = jnp.sum(jnp.where((lane16 == target) & (sub < 12), packed, 0.0), axis=0, keepdims=True)
    sent[...] = jnp.broadcast_to(row, sent.shape)


def relay(received, sent):
    sent[...] = jnp.broadcast_to(jnp.sum(received[...], axis=0, keepdims=True), sent.shape)


def coefficients(nu):
    def inner(a, b, lift):
        total = None
        for i, x in enumerate(a):
            for j, y in enumerate(b):
                term = (x * y) * nu[i + j + lift]
                total = term if total is None else total + term
        return total

    residual = [jnp.ones_like(nu[0])]
    direction = residual
    answer = []
    norm = nu[0]
    for iteration in range(3):
        energy = SHIFT * inner(direction, direction, 0) + SPAN * inner(direction, direction, 1)
        step = jnp.clip(norm / energy, STEP_LOW, 1.0)
        answer = [a + step * d for a, d in zip(answer + [0.0], direction)]
        if iteration == 2:
            return answer
        image = [SHIFT * d for d in direction] + [0.0]
        image = [i + SPAN * d for i, d in zip(image, [0.0] + direction)]
        residual = [r - step * i for r, i in zip(residual + [0.0], image)]
        new = jnp.maximum(inner(residual, residual, 0), 0.0)
        ratio = new / norm
        direction = [r + ratio * d for r, d in zip(residual, direction + [0.0])]
        norm = new


def finish(received, basis, pots, adjoint, gradient, field):
    depth = basis.shape[2]
    row = jnp.sum(received[...], axis=0, keepdims=True)
    row = jnp.broadcast_to(row, (8, 128))
    combined = coefficients([roll(row, -i, 1) for i in range(6)])
    lane = lanes_of()
    scale = [
        [
            jnp.sum(jnp.where(lane == k * SECOND, c, 0.0), axis=1, keepdims=True)[0:1, 0:1]
            for c in combined
        ]
        for k in range(2)
    ]
    for k in range(2):
        c = [jnp.broadcast_to(x, (16, 256)) for x in scale[k]]
        for z in range(depth):
            value = c[0] * basis[0, k, z] + c[1] * basis[1, k, z] + c[2] * basis[2, k, z]
            field[k, z] = value
            adjoint[k, z] = value[0:8, 0:128]
    carry = None
    for z in range(depth):
        gx = gy = gz = None
        for k in range(2):
            a, p = field[k, z], pots[k, z]
            tx = (a - roll(a, -1, 0)) * (p - roll(p, -1, 0))
            ty = (a - roll(a, -1, 1)) * (p - roll(p, -1, 1))
            gx = tx if gx is None else gx + tx
            gy = ty if gy is None else gy + ty
            if z + 1 < depth:
                tz = (a[0:8, 0:128] - field[k, z + 1, 0:8, 0:128]) * (
                    p[0:8, 0:128] - pots[k, z + 1, 0:8, 0:128]
                )
                gz = tz if gz is None else gz + tz
        total = (gx + roll(gx, 1, 0) + gy + roll(gy, 1, 1))[0:8, 0:128]
        if carry is not None:
            total = total + carry
        if gz is not None:
            total = total + gz
        carry = gz
        gradient[z] = -0.5 * total


def local(body, outs, scratch=(), space=pltpu.VMEM, limit=32 * 2**20, kind=pltpu.VMEM):
    vmem = pl.BlockSpec(memory_space=pltpu.VMEM)
    shapes = [kind(s, jnp.float32) for s in outs]

    def call(*args):
        return pl.pallas_call(
            body,
            out_shape=shapes,
            in_specs=[pl.BlockSpec(memory_space=space)] * len(args),
            out_specs=[vmem] * len(outs),
            scratch_shapes=list(scratch),
            compiler_params=pltpu.CompilerParams(vmem_limit_bytes=limit),
        )(*args)

    return call


def scratch(*shape, dtype=jnp.float32):
    return pltpu.VMEM(shape, dtype)


def trade(x, axis, start):
    pairs = [(i, i + 1) for i in range(start, lax.axis_size(axis) - 1, 2)]
    return lax.ppermute(x, axis, pairs + [(j, i) for i, j in pairs])


def per_device(conductance, labels, cotangent, saved):
    depth = conductance.shape[0]
    rows, cols = lax.axis_size("gx"), lax.axis_size("gy")
    args = (conductance, labels, cotangent, saved)
    tiles = depth * GROUP // 128
    first, second, field = local(
        pack_columns,
        [(tiles, 8, 128)] * 2 + [(6, depth, 8, 128)],
        [scratch(*x.shape, dtype=x.dtype) for x in args] + [pltpu.SemaphoreType.DMA((4,))],
        pltpu.HBM,
        56 * 2**20,
    )(*args)
    first, second = trade(first, "gy", 0), trade(second, "gy", 1)
    wide, near, far = local(widen, [(6, depth, 8, 256)] + [(depth + 1, 16, 128)] * 2)(
        field, first, second
    )
    far = trade(far, "gx", 1)
    near = lax.all_gather(near, "gx", axis_index_groups=[[i, i + 1] for i in range(0, rows, 2)])
    sent, basis, pots = local(
        moments,
        [(rows, 128), (3, 2, depth, 16, 256), (2, depth, 16, 256)],
        [scratch(1, depth, 16, 256), scratch(4, depth, 16, 256), scratch(2, depth, 16, 256)],
    )(wide, near, far)
    received = lax.all_to_all(sent, "gx", 0, 0, tiled=True)
    (sent,) = local(relay, [(cols, 128)])(received)
    received = lax.all_to_all(sent, "gy", 0, 0, tiled=True)
    adjoint, gradient = local(
        finish, [cotangent.shape, conductance.shape], [scratch(2, depth, 16, 256)],
        kind=jax.ShapeDtypeStruct,
    )(received, basis, pots)
    return adjoint, gradient


def solution(mesh):
    return jax.shard_map(
        per_device,
        mesh=mesh,
        in_specs=(
            P(None, "gx", "gy"),
            P(None, "gx", "gy"),
            P(None, None, "gx", "gy"),
            P(None, None, "gx", "gy"),
        ),
        out_specs=(P(None, None, "gx", "gy"), P(None, "gx", "gy")),
        check_vma=False,
    )
```

```python
import jax
import jax.numpy as jnp
from jax import lax
from jax.experimental import pallas as pl
from jax.experimental.pallas import tpu as pltpu
from jax.sharding import PartitionSpec as P

SHIFT = 2.0
SPAN = 32.0
STEP_LOW = 1.0 / 61.0
SECOND = 64
COND, MASK, RES1, RES2, POT1, POT2 = range(6)
WIDTH = (3, 2, 3, 3, 1, 1)
LANE = (0, 9, 3, 6, 11, 12)
SLOT = (0, 6, 3, 8, 11, 12)
GROUP = 16


def roll(x, amount, axis):
    amount = amount % x.shape[axis]
    return x if amount == 0 else pltpu.roll(x, amount, axis)


def fields_at(cond, labels, cot, saved, z):
    tag = labels[z]
    free = tag == 0
    mask = jnp.where(free, 1.0, 0.0)
    pots = [jnp.where(tag == k + 1, 1.0, jnp.where(free, saved[k, z], 0.0)) for k in range(2)]
    return [cond[z], mask] + [jnp.where(free, cot[k, z], 0.0) for k in range(2)] + pots


def lanes_of(shape=(8, 128)):
    return lax.broadcasted_iota(jnp.int32, shape, 1)


def within(index, low, count):
    return (index >= low) & (index < low + count)


def exact_dot(x, matrix):
    total = None
    for _ in range(3):
        term = x.astype(jnp.bfloat16)
        x = x - term.astype(jnp.float32)
        part = jnp.dot(term, matrix, preferred_element_type=jnp.float32)
        total = part if total is None else total + part
    return total


def difference_matrices():
    i = lax.broadcasted_iota(jnp.int32, (256, 256), 0)
    j = lax.broadcasted_iota(jnp.int32, (256, 256), 1)
    here = jnp.where(i == j, 1.0, 0.0)
    forward = here - jnp.where(i == (j + 1) % 256, 1.0, 0.0)
    backward = here - jnp.where((i + 1) % 256 == j, 1.0, 0.0)
    return forward.astype(jnp.bfloat16), backward.astype(jnp.bfloat16)


def place(shape, rows, cols, pairs):
    i = lax.broadcasted_iota(jnp.int32, shape, rows)
    j = lax.broadcasted_iota(jnp.int32, shape, cols)
    hit = i < 0
    for row, col, count in pairs:
        hit |= within(i, row, count) & (j - i == col - row)
    return jnp.where(hit, 1.0, 0.0).astype(jnp.bfloat16)


def pack_columns(cond_in, labels_in, cot_in, saved_in, first, second, field, cond, labels, cot, saved, sems):
    copies = [
        pltpu.make_async_copy(source, target, sems.at[i])
        for i, (source, target) in enumerate(
            ((cond_in, cond), (labels_in, labels), (cot_in, cot), (saved_in, saved))
        )
    ]
    for copy in copies:
        copy.start()
    picks = [
        place(
            (128, 128),
            0,
            1,
            [(0, LANE[f], WIDTH[f]), (128 - WIDTH[f], GROUP + LANE[f], WIDTH[f])],
        )
        for f in range(6)
    ]
    for copy in copies:
        copy.wait()
    even = lax.axis_index("gy") % 2 == 0
    depth = cond.shape[0]
    for z in range(depth):
        for f, x in enumerate(fields_at(cond, labels, cot, saved, z)):
            field[f, z] = x
    total = None
    for f in range(6):
        part = exact_dot(field[f].reshape(depth * 8, 128), picks[f])
        total = part if total is None else total + part
    columns = total.T
    left, right = columns[0:GROUP], columns[GROUP : 2 * GROUP]
    first[...] = jnp.where(even, right, left)
    second[...] = jnp.where(even, left, right)


def unpack_columns(left, right, out):
    packed = jnp.concatenate([left, right], axis=0).T
    for f in range(6):
        w = WIDTH[f]
        matrix = place(
            (2 * GROUP, 128), 0, 1, [(LANE[f], 128 - w, w), (GROUP + LANE[f], 0, w)]
        )
        out[:, f * 128 : (f + 1) * 128] = exact_dot(packed, matrix)


def widen(field, sent_first, sent_second, from_first, from_second, wide, near, far, halo):
    even = lax.axis_index("gy") % 2 == 0
    upper = lax.axis_index("gx") % 2 == 0
    depth = field.shape[1]
    slot = lax.broadcasted_iota(jnp.int32, (GROUP, 128), 0)
    c = LANE[COND]

    def choose(a, b):
        return jnp.where(even, a[...], b[...])

    left, right = choose(from_second, from_first), choose(from_first, from_second)
    own_left, own_right = choose(sent_second, sent_first), choose(sent_first, sent_second)
    pot = (slot == LANE[POT1]) | (slot == LANE[POT2])
    outside = right[c : c + 1] == 0.0
    right = jnp.where(outside & (slot == c), -roll(own_right, -2, 0), right)
    right = jnp.where(outside & pot, own_right, right)
    outside = left[c + 2 : c + 3] == 0.0
    left = jnp.where(outside & (slot == c + 2), -roll(own_left, 2, 0), left)
    left = jnp.where(outside & pot, own_left, left)
    near[depth] = left
    near[depth + 1] = right
    far[depth] = left
    far[depth + 1] = right
    unpack_columns(left, right, halo)
    for z in range(depth):
        fields = [field[f, z] for f in range(6)]
        for f in range(6):
            wide[f, z, :, 0:128] = fields[f]
            wide[f, z, :, 128:256] = halo[8 * z : 8 * z + 8, f * 128 : (f + 1) * 128]
        own = []
        for side in range(2):
            rows = []
            for f in (COND, RES1, MASK, RES2, POT1, POT2):
                w = WIDTH[f]
                start = 0 if side == 0 else 8 - w
                rows.append(fields[f][start : start + w])
            own.append(jnp.concatenate(rows + [jnp.zeros((3, 128), jnp.float32)], axis=0))
        near[z] = jnp.where(upper, own[1], own[0])
        far[z] = jnp.where(upper, own[0], own[1])


def moments(wide, from_near, from_far, sent, basis, pots, field, weight, flux, corner):
    depth = wide.shape[1]
    core = lax.axis_index("gx") % 2
    lane16 = lanes_of((16, 128))
    row8 = lax.broadcasted_iota(jnp.int32, (8, 256), 0)

    def above(i):
        return jnp.where(core == 0, from_far[i], from_near[1 - core, i])

    def below(i):
        return jnp.where(core == 0, from_near[1 - core, i], from_far[i])

    for side, source in enumerate((above, below)):
        unpack_columns(source(depth), source(depth + 1), corner.at[side])
    for z in range(depth):
        top, bottom = above(z), below(z)
        parts = []
        for f in range(6):
            w, s = WIDTH[f], SLOT[f]
            own = wide[f, z]
            gap = jnp.zeros((8 - 2 * w, 128), jnp.float32)
            low = jnp.concatenate([bottom[s : s + w], gap, top[s : s + w]], axis=0)
            tips = [
                corner[side, 8 * z : 8 * z + 8, f * 128 : (f + 1) * 128] for side in range(2)
            ]
            high = jnp.concatenate([tips[1][0:w], gap, tips[0][8 - w : 8]], axis=0)
            parts.append((own, jnp.concatenate([low, high], axis=1)))
        own, other = parts[COND]
        outside = (other == 0.0) & ((row8 == 0) | (row8 == 7))

        def edge_value(x):
            return jnp.where(row8 == 0, roll(x, 1, 0), roll(x, -1, 0))

        parts[COND] = (own, jnp.where(outside, -edge_value(own), other))
        for f in (POT1, POT2):
            own, other = parts[f]
            parts[f] = (own, jnp.where(outside, edge_value(own), other))
        field[0, z, 0:8], field[0, z, 8:16] = parts[COND]
        weight[3, z, 0:8] = parts[MASK][0] * (1.0 / SPAN)
        weight[3, z, 8:16] = parts[MASK][1] * (1.0 / SPAN)
        for k in range(2):
            basis[0, k, z, 0:8], basis[0, k, z, 8:16] = parts[RES1 + k]
            pots[k, z, 0:8], pots[k, z, 8:16] = parts[POT1 + k]
    for z in range(depth):
        c = field[0, z]
        weight[0, z] = 0.5 * (c + roll(c, -1, 0))
        weight[1, z] = 0.5 * (c + roll(c, -1, 1))
        if z + 1 < depth:
            weight[2, z] = 0.5 * (c + field[0, z + 1])

    forward, backward = difference_matrices()

    def image(k, z, source, carry):
        u = basis[source, k, z]
        fx = weight[0, z] * (u - roll(u, -1, 0))
        total = (fx - roll(fx, 1, 0)) + flux[k, z] - u
        if carry is not None:
            total = total - carry
        carry = None
        if z + 1 < depth:
            carry = weight[2, z] * (u - basis[source, k, z + 1])
            total = total + carry
        return weight[3, z] * total, carry

    def lane_fluxes(source, rows):
        for k in range(2):
            u = basis[source, k, :, 0:rows].reshape(depth * rows, 256)
            f = weight[1, :, 0:rows].reshape(depth * rows, 256) * exact_dot(u, forward)
            flux[k, :, 0:rows] = exact_dot(f, backward).reshape(depth, rows, 256)

    for power in range(2):
        lane_fluxes(power, 16)
        for k in range(2):
            carry = None
            for z in range(depth):
                value, carry = image(k, z, power, carry)
                basis[power + 1, k, z] = value
    own = (slice(0, 8), slice(0, 128))

    def own_image(k, z, carry):
        u = basis[2, k, z, :, 0:128]
        fx = weight[0, z, :, 0:128] * (u - roll(u, -1, 0))
        u = u[0:8]
        total = (fx - roll(fx, 1, 0))[0:8] + flux[k, z, 0:8, 0:128] - u
        if carry is not None:
            total = total - carry
        carry = None
        if z + 1 < depth:
            carry = weight[2, z, 0:8, 0:128] * (u - basis[2, k, z + 1, 0:8, 0:128])
            total = total + carry
        return weight[3, z, 0:8, 0:128] * total, carry

    lane_fluxes(2, 8)
    totals = []
    for k in range(2):
        sums = [jnp.zeros((8, 128), jnp.float32) for _ in range(6)]
        carry = None
        for z in range(depth):
            last, carry = own_image(k, z, carry)
            v = [basis[i, k, z, 0:8, 0:128] for i in range(3)] + [last]
            sums = [s + v[i // 2] * v[i - i // 2] for i, s in enumerate(sums)]
        totals += sums
    sub = lax.broadcasted_iota(jnp.int32, (16, 128), 0)
    packed = jnp.zeros((16, 128), jnp.float32)
    for i, s in enumerate(totals):
        packed = jnp.where(sub == i, jnp.sum(s, axis=0, keepdims=True), packed)
    packed = jnp.sum(packed, axis=1, keepdims=True)
    target = jnp.where(sub < 6, sub, sub - 6 + SECOND)
    row = jnp.sum(jnp.where((lane16 == target) & (sub < 12), packed, 0.0), axis=0, keepdims=True)
    sent[...] = jnp.broadcast_to(row, sent.shape)


def relay(received, sent):
    sent[...] = jnp.broadcast_to(jnp.sum(received[...], axis=0, keepdims=True), sent.shape)


def coefficients(nu):
    def inner(a, b, lift):
        total = None
        for i, x in enumerate(a):
            for j, y in enumerate(b):
                term = (x * y) * nu[i + j + lift]
                total = term if total is None else total + term
        return total

    residual = [jnp.ones_like(nu[0])]
    direction = residual
    answer = []
    norm = nu[0]
    for iteration in range(3):
        energy = SHIFT * inner(direction, direction, 0) + SPAN * inner(direction, direction, 1)
        step = jnp.clip(norm / energy, STEP_LOW, 1.0)
        answer = [a + step * d for a, d in zip(answer + [0.0], direction)]
        if iteration == 2:
            return answer
        image = [SHIFT * d for d in direction] + [0.0]
        image = [i + SPAN * d for i, d in zip(image, [0.0] + direction)]
        residual = [r - step * i for r, i in zip(residual + [0.0], image)]
        new = jnp.maximum(inner(residual, residual, 0), 0.0)
        ratio = new / norm
        direction = [r + ratio * d for r, d in zip(residual, direction + [0.0])]
        norm = new


def finish(received, basis, pots, adjoint, gradient, field, lanes):
    depth = basis.shape[2]
    row = jnp.sum(received[...], axis=0, keepdims=True)
    row = jnp.broadcast_to(row, (8, 128))
    combined = coefficients([roll(row, -i, 1) for i in range(6)])
    lane = lanes_of()
    scale = [
        [
            jnp.sum(jnp.where(lane == k * SECOND, c, 0.0), axis=1, keepdims=True)[0:1, 0:1]
            for c in combined
        ]
        for k in range(2)
    ]
    for k in range(2):
        c = [jnp.broadcast_to(x, (16, 256)) for x in scale[k]]
        for z in range(depth):
            value = c[0] * basis[0, k, z] + c[1] * basis[1, k, z] + c[2] * basis[2, k, z]
            field[k, z] = value
            adjoint[k, z] = value[0:8, 0:128]
    forward, _ = difference_matrices()
    i = lax.broadcasted_iota(jnp.int32, (256, 256), 0)
    j = lax.broadcasted_iota(jnp.int32, (256, 256), 1)
    both = jnp.where((i == j) | ((i + 1) % 256 == j), 1.0, 0.0).astype(jnp.bfloat16)
    gy = None
    for k in range(2):
        a, p = (x[k, :, 0:8].reshape(depth * 8, 256) for x in (field, pots))
        term = exact_dot(a, forward) * exact_dot(p, forward)
        gy = term if gy is None else gy + term
    lanes[...] = exact_dot(gy, both[:, 0:128])
    carry = None
    for z in range(depth):
        gx = gz = None
        for k in range(2):
            a, p = field[k, z, :, 0:128], pots[k, z, :, 0:128]
            tx = (a - roll(a, -1, 0)) * (p - roll(p, -1, 0))
            gx = tx if gx is None else gx + tx
            if z + 1 < depth:
                tz = (a[0:8] - field[k, z + 1, 0:8, 0:128]) * (
                    p[0:8] - pots[k, z + 1, 0:8, 0:128]
                )
                gz = tz if gz is None else gz + tz
        total = (gx + roll(gx, 1, 0))[0:8] + lanes[8 * z : 8 * z + 8]
        if carry is not None:
            total = total + carry
        if gz is not None:
            total = total + gz
        carry = gz
        gradient[z] = -0.5 * total


def local(body, outs, scratch=(), space=pltpu.VMEM, limit=32 * 2**20, kind=pltpu.VMEM):
    vmem = pl.BlockSpec(memory_space=pltpu.VMEM)
    shapes = [kind(s, jnp.float32) for s in outs]

    def call(*args):
        return pl.pallas_call(
            body,
            out_shape=shapes,
            in_specs=[pl.BlockSpec(memory_space=space)] * len(args),
            out_specs=[vmem] * len(outs),
            scratch_shapes=list(scratch),
            compiler_params=pltpu.CompilerParams(vmem_limit_bytes=limit),
        )(*args)

    return call


def scratch(*shape, dtype=jnp.float32):
    return pltpu.VMEM(shape, dtype)


def trade(x, axis, start):
    pairs = [(i, i + 1) for i in range(start, lax.axis_size(axis) - 1, 2)]
    return lax.ppermute(x, axis, pairs + [(j, i) for i, j in pairs])


def per_device(conductance, labels, cotangent, saved):
    depth = conductance.shape[0]
    rows, cols = lax.axis_size("gx"), lax.axis_size("gy")
    args = (conductance, labels, cotangent, saved)
    first, second, field = local(
        pack_columns,
        [(GROUP, depth * 8)] * 2 + [(6, depth, 8, 128)],
        [scratch(*x.shape, dtype=x.dtype) for x in args] + [pltpu.SemaphoreType.DMA((4,))],
        pltpu.HBM,
        56 * 2**20,
    )(*args)
    from_first, from_second = trade(first, "gy", 0), trade(second, "gy", 1)
    wide, near, far = local(
        widen,
        [(6, depth, 8, 256)] + [(depth + 2, 16, 128)] * 2,
        [scratch(depth * 8, 768)],
    )(field, first, second, from_first, from_second)
    far = trade(far, "gx", 1)
    near = lax.all_gather(near, "gx", axis_index_groups=[[i, i + 1] for i in range(0, rows, 2)])
    sent, basis, pots = local(
        moments,
        [(rows, 128), (3, 2, depth, 16, 256), (2, depth, 16, 256)],
        [scratch(1, depth, 16, 256), scratch(4, depth, 16, 256), scratch(2, depth, 16, 256), scratch(2, depth * 8, 768)],
    )(wide, near, far)
    received = lax.all_to_all(sent, "gx", 0, 0, tiled=True)
    (sent,) = local(relay, [(cols, 128)])(received)
    received = lax.all_to_all(sent, "gy", 0, 0, tiled=True)
    adjoint, gradient = local(
        finish,
        [cotangent.shape, conductance.shape],
        [scratch(2, depth, 16, 256), scratch(depth * 8, 128)],
        kind=jax.ShapeDtypeStruct,
    )(received, basis, pots)
    return adjoint, gradient


def solution(mesh):
    return jax.shard_map(
        per_device,
        mesh=mesh,
        in_specs=(
            P(None, "gx", "gy"),
            P(None, "gx", "gy"),
            P(None, None, "gx", "gy"),
            P(None, None, "gx", "gy"),
        ),
        out_specs=(P(None, None, "gx", "gy"), P(None, "gx", "gy")),
        check_vma=False,
    )
```

```python
import jax
import jax.numpy as jnp
from jax import lax
from jax.experimental import pallas as pl
from jax.experimental.pallas import tpu as pltpu
from jax.sharding import PartitionSpec as P

SHIFT = 2.0
SPAN = 32.0
STEP_LOW = 1.0 / 61.0
SECOND = 64
COND, MASK, RES1, RES2, POT1, POT2 = range(6)
WIDTH = (3, 2, 3, 3, 1, 1)
LANE = (0, 9, 3, 6, 11, 12)
SLOT = (0, 6, 3, 8, 11, 12)
GROUP = 16


def roll(x, amount, axis):
    amount = amount % x.shape[axis]
    return x if amount == 0 else pltpu.roll(x, amount, axis)


def fields_at(cond, labels, cot, saved, z):
    tag = labels[z]
    free = tag == 0
    mask = jnp.where(free, 1.0, 0.0)
    pots = [jnp.where(tag == k + 1, 1.0, jnp.where(free, saved[k, z], 0.0)) for k in range(2)]
    return [cond[z], mask] + [jnp.where(free, cot[k, z], 0.0) for k in range(2)] + pots


def lanes_of(shape=(8, 128)):
    return lax.broadcasted_iota(jnp.int32, shape, 1)


def within(index, low, count):
    return (index >= low) & (index < low + count)


def exact_dot(x, matrix):
    total = None
    for _ in range(3):
        term = x.astype(jnp.bfloat16)
        x = x - term.astype(jnp.float32)
        part = jnp.dot(term, matrix, preferred_element_type=jnp.float32)
        total = part if total is None else total + part
    return total


def difference_matrices():
    i = lax.broadcasted_iota(jnp.int32, (256, 256), 0)
    j = lax.broadcasted_iota(jnp.int32, (256, 256), 1)
    here = jnp.where(i == j, 1.0, 0.0)
    forward = here - jnp.where(i == (j + 1) % 256, 1.0, 0.0)
    backward = here - jnp.where((i + 1) % 256 == j, 1.0, 0.0)
    return forward.astype(jnp.bfloat16), backward.astype(jnp.bfloat16)


def place(shape, rows, cols, pairs):
    i = lax.broadcasted_iota(jnp.int32, shape, rows)
    j = lax.broadcasted_iota(jnp.int32, shape, cols)
    hit = i < 0
    for row, col, count in pairs:
        hit |= within(i, row, count) & (j - i == col - row)
    return jnp.where(hit, 1.0, 0.0).astype(jnp.bfloat16)


def pack_columns(cond_in, labels_in, cot_in, saved_in, first, second, field, cond, labels, cot, saved, sems):
    copies = [
        pltpu.make_async_copy(source, target, sems.at[i])
        for i, (source, target) in enumerate(
            ((cond_in, cond), (labels_in, labels), (cot_in, cot), (saved_in, saved))
        )
    ]
    for copy in copies:
        copy.start()
    picks = [
        place(
            (128, 128),
            0,
            1,
            [(0, LANE[f], WIDTH[f]), (128 - WIDTH[f], GROUP + LANE[f], WIDTH[f])],
        )
        for f in range(6)
    ]
    for copy in copies:
        copy.wait()
    even = lax.axis_index("gy") % 2 == 0
    depth = cond.shape[0]
    for z in range(depth):
        for f, x in enumerate(fields_at(cond, labels, cot, saved, z)):
            field[f, z] = x
    total = None
    for f in range(6):
        part = exact_dot(field[f].reshape(depth * 8, 128), picks[f])
        total = part if total is None else total + part
    columns = total.T
    left, right = columns[0:GROUP], columns[GROUP : 2 * GROUP]
    first[...] = jnp.where(even, right, left)
    second[...] = jnp.where(even, left, right)


def unpack_columns(left, right, out):
    packed = jnp.concatenate([left, right], axis=0).T
    for f in range(6):
        w = WIDTH[f]
        matrix = place(
            (2 * GROUP, 128), 0, 1, [(LANE[f], 128 - w, w), (GROUP + LANE[f], 0, w)]
        )
        out[:, f * 128 : (f + 1) * 128] = exact_dot(packed, matrix)


def widen(field, sent_first, sent_second, from_second, from_first, wide, near, far, halo):
    even = lax.axis_index("gy") % 2 == 0
    upper = lax.axis_index("gx") % 2 == 0
    depth = field.shape[1]
    slot = lax.broadcasted_iota(jnp.int32, (GROUP, 128), 0)
    c = LANE[COND]

    def choose(a, b):
        return jnp.where(even, a[...], b[...])

    left, right = choose(from_second, from_first), choose(from_first, from_second)
    own_left, own_right = choose(sent_second, sent_first), choose(sent_first, sent_second)
    pot = (slot == LANE[POT1]) | (slot == LANE[POT2])
    outside = right[c : c + 1] == 0.0
    right = jnp.where(outside & (slot == c), -roll(own_right, -2, 0), right)
    right = jnp.where(outside & pot, own_right, right)
    outside = left[c + 2 : c + 3] == 0.0
    left = jnp.where(outside & (slot == c + 2), -roll(own_left, 2, 0), left)
    left = jnp.where(outside & pot, own_left, left)
    near[depth] = left
    near[depth + 1] = right
    far[depth] = left
    far[depth + 1] = right
    unpack_columns(left, right, halo)
    for z in range(depth):
        fields = [field[f, z] for f in range(6)]
        for f in range(6):
            wide[f, z, :, 0:128] = fields[f]
            wide[f, z, :, 128:256] = halo[8 * z : 8 * z + 8, f * 128 : (f + 1) * 128]
        own = []
        for side in range(2):
            rows = []
            for f in (COND, RES1, MASK, RES2, POT1, POT2):
                w = WIDTH[f]
                start = 0 if side == 0 else 8 - w
                rows.append(fields[f][start : start + w])
            own.append(jnp.concatenate(rows + [jnp.zeros((3, 128), jnp.float32)], axis=0))
        near[z] = jnp.where(upper, own[1], own[0])
        far[z] = jnp.where(upper, own[0], own[1])


def moments(wide, from_near, from_far, sent, basis, pots, field, weight, flux, corner):
    depth = wide.shape[1]
    core = lax.axis_index("gx") % 2
    lane16 = lanes_of((16, 128))
    row8 = lax.broadcasted_iota(jnp.int32, (8, 256), 0)

    def above(i):
        return jnp.where(core == 0, from_far[i], from_near[1 - core, i])

    def below(i):
        return jnp.where(core == 0, from_near[1 - core, i], from_far[i])

    for side, source in enumerate((above, below)):
        unpack_columns(source(depth), source(depth + 1), corner.at[side])
    for z in range(depth):
        top, bottom = above(z), below(z)
        parts = []
        for f in range(6):
            w, s = WIDTH[f], SLOT[f]
            own = wide[f, z]
            gap = jnp.zeros((8 - 2 * w, 128), jnp.float32)
            low = jnp.concatenate([bottom[s : s + w], gap, top[s : s + w]], axis=0)
            tips = [
                corner[side, 8 * z : 8 * z + 8, f * 128 : (f + 1) * 128] for side in range(2)
            ]
            high = jnp.concatenate([tips[1][0:w], gap, tips[0][8 - w : 8]], axis=0)
            parts.append((own, jnp.concatenate([low, high], axis=1)))
        own, other = parts[COND]
        outside = (other == 0.0) & ((row8 == 0) | (row8 == 7))

        def edge_value(x):
            return jnp.where(row8 == 0, roll(x, 1, 0), roll(x, -1, 0))

        parts[COND] = (own, jnp.where(outside, -edge_value(own), other))
        for f in (POT1, POT2):
            own, other = parts[f]
            parts[f] = (own, jnp.where(outside, edge_value(own), other))
        field[0, z, 0:8], field[0, z, 8:16] = parts[COND]
        weight[3, z, 0:8] = parts[MASK][0] * (1.0 / SPAN)
        weight[3, z, 8:16] = parts[MASK][1] * (1.0 / SPAN)
        for k in range(2):
            basis[0, k, z, 0:8], basis[0, k, z, 8:16] = parts[RES1 + k]
            pots[k, z, 0:8], pots[k, z, 8:16] = parts[POT1 + k]
    for z in range(depth):
        c = field[0, z]
        weight[0, z] = 0.5 * (c + roll(c, -1, 0))
        weight[1, z] = 0.5 * (c + roll(c, -1, 1))
        if z + 1 < depth:
            weight[2, z] = 0.5 * (c + field[0, z + 1])

    forward, backward = difference_matrices()

    def image(k, z, source, carry):
        u = basis[source, k, z]
        fx = weight[0, z] * (u - roll(u, -1, 0))
        total = (fx - roll(fx, 1, 0)) + flux[k, z] - u
        if carry is not None:
            total = total - carry
        carry = None
        if z + 1 < depth:
            carry = weight[2, z] * (u - basis[source, k, z + 1])
            total = total + carry
        return weight[3, z] * total, carry

    def lane_fluxes(source, rows):
        for k in range(2):
            u = basis[source, k, :, 0:rows].reshape(depth * rows, 256)
            f = weight[1, :, 0:rows].reshape(depth * rows, 256) * exact_dot(u, forward)
            flux[k, :, 0:rows] = exact_dot(f, backward).reshape(depth, rows, 256)

    for power in range(2):
        lane_fluxes(power, 16)
        for k in range(2):
            carry = None
            for z in range(depth):
                value, carry = image(k, z, power, carry)
                basis[power + 1, k, z] = value
    own = (slice(0, 8), slice(0, 128))

    def own_image(k, z, carry):
        u = basis[2, k, z, :, 0:128]
        fx = weight[0, z, :, 0:128] * (u - roll(u, -1, 0))
        u = u[0:8]
        total = (fx - roll(fx, 1, 0))[0:8] + flux[k, z, 0:8, 0:128] - u
        if carry is not None:
            total = total - carry
        carry = None
        if z + 1 < depth:
            carry = weight[2, z, 0:8, 0:128] * (u - basis[2, k, z + 1, 0:8, 0:128])
            total = total + carry
        return weight[3, z, 0:8, 0:128] * total, carry

    lane_fluxes(2, 8)
    totals = []
    for k in range(2):
        sums = [jnp.zeros((8, 128), jnp.float32) for _ in range(6)]
        carry = None
        for z in range(depth):
            last, carry = own_image(k, z, carry)
            v = [basis[i, k, z, 0:8, 0:128] for i in range(3)] + [last]
            sums = [s + v[i // 2] * v[i - i // 2] for i, s in enumerate(sums)]
        totals += sums
    sub = lax.broadcasted_iota(jnp.int32, (16, 128), 0)
    packed = jnp.zeros((16, 128), jnp.float32)
    for i, s in enumerate(totals):
        packed = jnp.where(sub == i, jnp.sum(s, axis=0, keepdims=True), packed)
    packed = jnp.sum(packed, axis=1, keepdims=True)
    target = jnp.where(sub < 6, sub, sub - 6 + SECOND)
    row = jnp.sum(jnp.where((lane16 == target) & (sub < 12), packed, 0.0), axis=0, keepdims=True)
    sent[...] = jnp.broadcast_to(row, sent.shape)


def relay(received, sent):
    sent[...] = jnp.broadcast_to(jnp.sum(received[...], axis=0, keepdims=True), sent.shape)


def coefficients(nu):
    def inner(a, b, lift):
        total = None
        for i, x in enumerate(a):
            for j, y in enumerate(b):
                term = (x * y) * nu[i + j + lift]
                total = term if total is None else total + term
        return total

    residual = [jnp.ones_like(nu[0])]
    direction = residual
    answer = []
    norm = nu[0]
    for iteration in range(3):
        energy = SHIFT * inner(direction, direction, 0) + SPAN * inner(direction, direction, 1)
        step = jnp.clip(norm / energy, STEP_LOW, 1.0)
        answer = [a + step * d for a, d in zip(answer + [0.0], direction)]
        if iteration == 2:
            return answer
        image = [SHIFT * d for d in direction] + [0.0]
        image = [i + SPAN * d for i, d in zip(image, [0.0] + direction)]
        residual = [r - step * i for r, i in zip(residual + [0.0], image)]
        new = jnp.maximum(inner(residual, residual, 0), 0.0)
        ratio = new / norm
        direction = [r + ratio * d for r, d in zip(residual, direction + [0.0])]
        norm = new


def finish(received, basis, pots, adjoint, gradient, field):
    depth = basis.shape[2]
    row = jnp.sum(received[...], axis=0, keepdims=True)
    row = jnp.broadcast_to(row, (8, 128))
    combined = coefficients([roll(row, -i, 1) for i in range(6)])
    lane = lanes_of()
    scale = [
        [
            jnp.sum(jnp.where(lane == k * SECOND, c, 0.0), axis=1, keepdims=True)[0:1, 0:1]
            for c in combined
        ]
        for k in range(2)
    ]
    for k in range(2):
        c = [jnp.broadcast_to(x, (16, 256)) for x in scale[k]]
        for z in range(depth):
            value = c[0] * basis[0, k, z] + c[1] * basis[1, k, z] + c[2] * basis[2, k, z]
            field[k, z] = value
            adjoint[k, z] = value[0:8, 0:128]
    carry = None
    for z in range(depth):
        gx = gy = gz = None
        for k in range(2):
            a, p = field[k, z], pots[k, z]
            tx = (a - roll(a, -1, 0)) * (p - roll(p, -1, 0))
            ty = (a - roll(a, -1, 1)) * (p - roll(p, -1, 1))
            gx = tx if gx is None else gx + tx
            gy = ty if gy is None else gy + ty
            if z + 1 < depth:
                tz = (a[0:8, 0:128] - field[k, z + 1, 0:8, 0:128]) * (
                    p[0:8, 0:128] - pots[k, z + 1, 0:8, 0:128]
                )
                gz = tz if gz is None else gz + tz
        total = (gx + roll(gx, 1, 0) + gy + roll(gy, 1, 1))[0:8, 0:128]
        if carry is not None:
            total = total + carry
        if gz is not None:
            total = total + gz
        carry = gz
        gradient[z] = -0.5 * total


def local(body, outs, scratch=(), space=pltpu.VMEM, limit=32 * 2**20, kind=pltpu.VMEM):
    vmem = pl.BlockSpec(memory_space=pltpu.VMEM)
    shapes = [kind(s, jnp.float32) for s in outs]

    def call(*args):
        return pl.pallas_call(
            body,
            out_shape=shapes,
            in_specs=[pl.BlockSpec(memory_space=space)] * len(args),
            out_specs=[vmem] * len(outs),
            scratch_shapes=list(scratch),
            compiler_params=pltpu.CompilerParams(vmem_limit_bytes=limit),
        )(*args)

    return call


def scratch(*shape, dtype=jnp.float32):
    return pltpu.VMEM(shape, dtype)


def trade(x, axis, start):
    pairs = [(i, i + 1) for i in range(start, lax.axis_size(axis) - 1, 2)]
    return lax.ppermute(x, axis, pairs + [(j, i) for i, j in pairs])


def per_device(conductance, labels, cotangent, saved):
    depth = conductance.shape[0]
    rows, cols = lax.axis_size("gx"), lax.axis_size("gy")
    args = (conductance, labels, cotangent, saved)
    first, second, field = local(
        pack_columns,
        [(GROUP, depth * 8)] * 2 + [(6, depth, 8, 128)],
        [scratch(*x.shape, dtype=x.dtype) for x in args] + [pltpu.SemaphoreType.DMA((4,))],
        pltpu.HBM,
        56 * 2**20,
    )(*args)
    from_second = trade(second, "gy", 1)
    from_first = trade(first, "gy", 0)
    wide, near, far = local(
        widen,
        [(6, depth, 8, 256)] + [(depth + 2, 16, 128)] * 2,
        [scratch(depth * 8, 768)],
    )(field, first, second, from_second, from_first)
    far = trade(far, "gx", 1)
    near = lax.all_gather(near, "gx", axis_index_groups=[[i, i + 1] for i in range(0, rows, 2)])
    sent, basis, pots = local(
        moments,
        [(rows, 128), (3, 2, depth, 16, 256), (2, depth, 16, 256)],
        [scratch(1, depth, 16, 256), scratch(4, depth, 16, 256), scratch(2, depth, 16, 256), scratch(2, depth * 8, 768)],
    )(wide, near, far)
    received = lax.all_to_all(sent, "gx", 0, 0, tiled=True)
    (sent,) = local(relay, [(cols, 128)])(received)
    received = lax.all_to_all(sent, "gy", 0, 0, tiled=True)
    adjoint, gradient = local(
        finish,
        [cotangent.shape, conductance.shape],
        [scratch(2, depth, 16, 256)],
        kind=jax.ShapeDtypeStruct,
    )(received, basis, pots)
    return adjoint, gradient


def solution(mesh):
    return jax.shard_map(
        per_device,
        mesh=mesh,
        in_specs=(
            P(None, "gx", "gy"),
            P(None, "gx", "gy"),
            P(None, None, "gx", "gy"),
            P(None, None, "gx", "gy"),
        ),
        out_specs=(P(None, None, "gx", "gy"), P(None, "gx", "gy")),
        check_vma=False,
    )
```

```python
import jax
import jax.numpy as jnp
from jax import lax
from jax.experimental import pallas as pl
from jax.experimental.pallas import tpu as pltpu
from jax.sharding import PartitionSpec as P

SHIFT = 2.0
SPAN = 32.0
STEP_LOW = 1.0 / 61.0
SECOND = 64
COND, MASK, RES1, RES2, POT1, POT2 = range(6)
WIDTH = (3, 2, 3, 3, 1, 1)
LANE = (0, 9, 3, 6, 11, 12)
SLOT = (0, 6, 3, 8, 11, 12)
GROUP = 16


def roll(x, amount, axis):
    amount = amount % x.shape[axis]
    return x if amount == 0 else pltpu.roll(x, amount, axis)


def fields_at(cond, labels, cot, saved, z):
    tag = labels[z]
    free = tag == 0
    mask = jnp.where(free, 1.0, 0.0)
    pots = [jnp.where(tag == k + 1, 1.0, jnp.where(free, saved[k, z], 0.0)) for k in range(2)]
    return [cond[z], mask] + [jnp.where(free, cot[k, z], 0.0) for k in range(2)] + pots


def lanes_of(shape=(8, 128)):
    return lax.broadcasted_iota(jnp.int32, shape, 1)


def within(index, low, count):
    return (index >= low) & (index < low + count)


def exact_dot(x, matrix):
    total = None
    for _ in range(3):
        term = x.astype(jnp.bfloat16)
        x = x - term.astype(jnp.float32)
        part = jnp.dot(term, matrix, preferred_element_type=jnp.float32)
        total = part if total is None else total + part
    return total


def difference_matrices():
    i = lax.broadcasted_iota(jnp.int32, (256, 256), 0)
    j = lax.broadcasted_iota(jnp.int32, (256, 256), 1)
    here = jnp.where(i == j, 1.0, 0.0)
    forward = here - jnp.where(i == (j + 1) % 256, 1.0, 0.0)
    backward = here - jnp.where((i + 1) % 256 == j, 1.0, 0.0)
    return forward.astype(jnp.bfloat16), backward.astype(jnp.bfloat16)


def place(shape, rows, cols, pairs):
    i = lax.broadcasted_iota(jnp.int32, shape, rows)
    j = lax.broadcasted_iota(jnp.int32, shape, cols)
    hit = i < 0
    for row, col, count in pairs:
        hit |= within(i, row, count) & (j - i == col - row)
    return jnp.where(hit, 1.0, 0.0).astype(jnp.bfloat16)


def pack_columns(cond_in, labels_in, cot_in, saved_in, first, second, field, cond, labels, cot, saved, sems):
    copies = [
        pltpu.make_async_copy(source, target, sems.at[i])
        for i, (source, target) in enumerate(
            ((cond_in, cond), (labels_in, labels), (cot_in, cot), (saved_in, saved))
        )
    ]
    for copy in copies:
        copy.start()
    picks = [
        place(
            (128, 128),
            0,
            1,
            [(0, LANE[f], WIDTH[f]), (128 - WIDTH[f], GROUP + LANE[f], WIDTH[f])],
        )
        for f in range(6)
    ]
    for copy in copies:
        copy.wait()
    even = lax.axis_index("gy") % 2 == 0
    depth = cond.shape[0]
    for z in range(depth):
        for f, x in enumerate(fields_at(cond, labels, cot, saved, z)):
            field[f, z] = x
    total = None
    for f in range(6):
        part = exact_dot(field[f].reshape(depth * 8, 128), picks[f])
        total = part if total is None else total + part
    columns = total.T
    left, right = columns[0:GROUP], columns[GROUP : 2 * GROUP]
    first[...] = jnp.where(even, right, left)
    second[...] = jnp.where(even, left, right)


def unpack_columns(columns, out):
    packed = columns.T
    for f in range(6):
        w = WIDTH[f]
        matrix = place(
            (2 * GROUP, 128), 0, 1, [(LANE[f], 128 - w, w), (GROUP + LANE[f], 0, w)]
        )
        out[:, f * 128 : (f + 1) * 128] = exact_dot(packed, matrix)


def pack_rows(field, first_in, first, near, far):
    first[...] = first_in[...]
    upper = lax.axis_index("gx") % 2 == 0
    for z in range(field.shape[1]):
        own = []
        for side in range(2):
            rows = []
            for f in (COND, RES1, MASK, RES2, POT1, POT2):
                w = WIDTH[f]
                start = 0 if side == 0 else 8 - w
                rows.append(field[f, z, start : start + w])
            own.append(jnp.concatenate(rows + [jnp.zeros((3, 128), jnp.float32)], axis=0))
        near[z] = jnp.where(upper, own[1], own[0])
        far[z] = jnp.where(upper, own[0], own[1])


def close_columns(sent_first, sent_second, from_first, from_second, after, columns):
    even = lax.axis_index("gy") % 2 == 0
    slot = lax.broadcasted_iota(jnp.int32, (GROUP, 128), 0)
    c = LANE[COND]

    def choose(a, b):
        return jnp.where(even, a[...], b[...])

    left, right = choose(from_second, from_first), choose(from_first, from_second)
    own_left, own_right = choose(sent_second, sent_first), choose(sent_first, sent_second)
    pot = (slot == LANE[POT1]) | (slot == LANE[POT2])
    outside = right[c : c + 1] == 0.0
    right = jnp.where(outside & (slot == c), -roll(own_right, -2, 0), right)
    right = jnp.where(outside & pot, own_right, right)
    outside = left[c + 2 : c + 3] == 0.0
    left = jnp.where(outside & (slot == c + 2), -roll(own_left, 2, 0), left)
    left = jnp.where(outside & pot, own_left, left)
    columns[0:GROUP] = left
    columns[GROUP : 2 * GROUP] = right


def widen(columns, halo):
    unpack_columns(columns[...], halo)


def moments(field_in, halo, near_rows, far_rows, near_columns, far_columns, sent, basis, pots, field, weight, flux, corner):
    depth = field_in.shape[1]
    core = lax.axis_index("gx") % 2
    lane16 = lanes_of((16, 128))
    row8 = lax.broadcasted_iota(jnp.int32, (8, 256), 0)

    def above(near, far):
        return jnp.where(core == 0, far, near)

    def below(near, far):
        return jnp.where(core == 0, near, far)

    for side, choose in enumerate((above, below)):
        unpack_columns(choose(near_columns[1 - core], far_columns[...]), corner.at[side])
    for z in range(depth):
        pair = near_rows[1 - core, z], far_rows[z]
        top, bottom = above(*pair), below(*pair)
        parts = []
        for f in range(6):
            w, s = WIDTH[f], SLOT[f]
            own = jnp.concatenate(
                [field_in[f, z], halo[8 * z : 8 * z + 8, f * 128 : (f + 1) * 128]], axis=1
            )
            gap = jnp.zeros((8 - 2 * w, 128), jnp.float32)
            low = jnp.concatenate([bottom[s : s + w], gap, top[s : s + w]], axis=0)
            tips = [
                corner[side, 8 * z : 8 * z + 8, f * 128 : (f + 1) * 128] for side in range(2)
            ]
            high = jnp.concatenate([tips[1][0:w], gap, tips[0][8 - w : 8]], axis=0)
            parts.append((own, jnp.concatenate([low, high], axis=1)))
        own, other = parts[COND]
        outside = (other == 0.0) & ((row8 == 0) | (row8 == 7))

        def edge_value(x):
            return jnp.where(row8 == 0, roll(x, 1, 0), roll(x, -1, 0))

        parts[COND] = (own, jnp.where(outside, -edge_value(own), other))
        for f in (POT1, POT2):
            own, other = parts[f]
            parts[f] = (own, jnp.where(outside, edge_value(own), other))
        field[0, z, 0:8], field[0, z, 8:16] = parts[COND]
        weight[3, z, 0:8] = parts[MASK][0] * (1.0 / SPAN)
        weight[3, z, 8:16] = parts[MASK][1] * (1.0 / SPAN)
        for k in range(2):
            basis[0, k, z, 0:8], basis[0, k, z, 8:16] = parts[RES1 + k]
            pots[k, z, 0:8], pots[k, z, 8:16] = parts[POT1 + k]
    for z in range(depth):
        c = field[0, z]
        weight[0, z] = 0.5 * (c + roll(c, -1, 0))
        weight[1, z] = 0.5 * (c + roll(c, -1, 1))
        if z + 1 < depth:
            weight[2, z] = 0.5 * (c + field[0, z + 1])

    forward, backward = difference_matrices()

    def image(k, z, source, carry):
        u = basis[source, k, z]
        fx = weight[0, z] * (u - roll(u, -1, 0))
        total = (fx - roll(fx, 1, 0)) + flux[k, z] - u
        if carry is not None:
            total = total - carry
        carry = None
        if z + 1 < depth:
            carry = weight[2, z] * (u - basis[source, k, z + 1])
            total = total + carry
        return weight[3, z] * total, carry

    def lane_fluxes(source, rows):
        for k in range(2):
            u = basis[source, k, :, 0:rows].reshape(depth * rows, 256)
            f = weight[1, :, 0:rows].reshape(depth * rows, 256) * exact_dot(u, forward)
            flux[k, :, 0:rows] = exact_dot(f, backward).reshape(depth, rows, 256)

    for power in range(2):
        lane_fluxes(power, 16)
        for k in range(2):
            carry = None
            for z in range(depth):
                value, carry = image(k, z, power, carry)
                basis[power + 1, k, z] = value
    own = (slice(0, 8), slice(0, 128))

    def own_image(k, z, carry):
        u = basis[2, k, z, :, 0:128]
        fx = weight[0, z, :, 0:128] * (u - roll(u, -1, 0))
        u = u[0:8]
        total = (fx - roll(fx, 1, 0))[0:8] + flux[k, z, 0:8, 0:128] - u
        if carry is not None:
            total = total - carry
        carry = None
        if z + 1 < depth:
            carry = weight[2, z, 0:8, 0:128] * (u - basis[2, k, z + 1, 0:8, 0:128])
            total = total + carry
        return weight[3, z, 0:8, 0:128] * total, carry

    lane_fluxes(2, 8)
    totals = []
    for k in range(2):
        sums = [jnp.zeros((8, 128), jnp.float32) for _ in range(6)]
        carry = None
        for z in range(depth):
            last, carry = own_image(k, z, carry)
            v = [basis[i, k, z, 0:8, 0:128] for i in range(3)] + [last]
            sums = [s + v[i // 2] * v[i - i // 2] for i, s in enumerate(sums)]
        totals += sums
    sub = lax.broadcasted_iota(jnp.int32, (16, 128), 0)
    packed = jnp.zeros((16, 128), jnp.float32)
    for i, s in enumerate(totals):
        packed = jnp.where(sub == i, jnp.sum(s, axis=0, keepdims=True), packed)
    packed = jnp.sum(packed, axis=1, keepdims=True)
    target = jnp.where(sub < 6, sub, sub - 6 + SECOND)
    row = jnp.sum(jnp.where((lane16 == target) & (sub < 12), packed, 0.0), axis=0, keepdims=True)
    sent[...] = jnp.broadcast_to(row, sent.shape)


def relay(received, sent):
    sent[...] = jnp.broadcast_to(jnp.sum(received[...], axis=0, keepdims=True), sent.shape)


def coefficients(nu):
    def inner(a, b, lift):
        total = None
        for i, x in enumerate(a):
            for j, y in enumerate(b):
                term = (x * y) * nu[i + j + lift]
                total = term if total is None else total + term
        return total

    residual = [jnp.ones_like(nu[0])]
    direction = residual
    answer = []
    norm = nu[0]
    for iteration in range(3):
        energy = SHIFT * inner(direction, direction, 0) + SPAN * inner(direction, direction, 1)
        step = jnp.clip(norm / energy, STEP_LOW, 1.0)
        answer = [a + step * d for a, d in zip(answer + [0.0], direction)]
        if iteration == 2:
            return answer
        image = [SHIFT * d for d in direction] + [0.0]
        image = [i + SPAN * d for i, d in zip(image, [0.0] + direction)]
        residual = [r - step * i for r, i in zip(residual + [0.0], image)]
        new = jnp.maximum(inner(residual, residual, 0), 0.0)
        ratio = new / norm
        direction = [r + ratio * d for r, d in zip(residual, direction + [0.0])]
        norm = new


def finish(received, basis, pots, adjoint, gradient, field):
    depth = basis.shape[2]
    row = jnp.sum(received[...], axis=0, keepdims=True)
    row = jnp.broadcast_to(row, (8, 128))
    combined = coefficients([roll(row, -i, 1) for i in range(6)])
    lane = lanes_of()
    scale = [
        [
            jnp.sum(jnp.where(lane == k * SECOND, c, 0.0), axis=1, keepdims=True)[0:1, 0:1]
            for c in combined
        ]
        for k in range(2)
    ]
    for k in range(2):
        c = [jnp.broadcast_to(x, (16, 256)) for x in scale[k]]
        for z in range(depth):
            value = c[0] * basis[0, k, z] + c[1] * basis[1, k, z] + c[2] * basis[2, k, z]
            field[k, z] = value
            adjoint[k, z] = value[0:8, 0:128]
    carry = None
    for z in range(depth):
        gx = gy = gz = None
        for k in range(2):
            a, p = field[k, z], pots[k, z]
            tx = (a - roll(a, -1, 0)) * (p - roll(p, -1, 0))
            ty = (a - roll(a, -1, 1)) * (p - roll(p, -1, 1))
            gx = tx if gx is None else gx + tx
            gy = ty if gy is None else gy + ty
            if z + 1 < depth:
                tz = (a[0:8, 0:128] - field[k, z + 1, 0:8, 0:128]) * (
                    p[0:8, 0:128] - pots[k, z + 1, 0:8, 0:128]
                )
                gz = tz if gz is None else gz + tz
        total = (gx + roll(gx, 1, 0) + gy + roll(gy, 1, 1))[0:8, 0:128]
        if carry is not None:
            total = total + carry
        if gz is not None:
            total = total + gz
        carry = gz
        gradient[z] = -0.5 * total


def local(body, outs, scratch=(), space=pltpu.VMEM, limit=32 * 2**20, kind=pltpu.VMEM):
    vmem = pl.BlockSpec(memory_space=pltpu.VMEM)
    shapes = [kind(s, jnp.float32) for s in outs]

    def call(*args):
        return pl.pallas_call(
            body,
            out_shape=shapes,
            in_specs=[pl.BlockSpec(memory_space=space)] * len(args),
            out_specs=[vmem] * len(outs),
            scratch_shapes=list(scratch),
            compiler_params=pltpu.CompilerParams(vmem_limit_bytes=limit),
        )(*args)

    return call


def scratch(*shape, dtype=jnp.float32):
    return pltpu.VMEM(shape, dtype)


def trade(x, axis, start):
    pairs = [(i, i + 1) for i in range(start, lax.axis_size(axis) - 1, 2)]
    return lax.ppermute(x, axis, pairs + [(j, i) for i, j in pairs])


def per_device(conductance, labels, cotangent, saved):
    depth = conductance.shape[0]
    rows, cols = lax.axis_size("gx"), lax.axis_size("gy")
    args = (conductance, labels, cotangent, saved)
    first, second, field = local(
        pack_columns,
        [(GROUP, depth * 8)] * 2 + [(6, depth, 8, 128)],
        [scratch(*x.shape, dtype=x.dtype) for x in args] + [pltpu.SemaphoreType.DMA((4,))],
        pltpu.HBM,
        56 * 2**20,
    )(*args)
    from_second = trade(second, "gy", 1)
    first, near, far = local(pack_rows, [(GROUP, depth * 8)] + [(depth, 16, 128)] * 2)(field, first)
    from_first = trade(first, "gy", 0)
    chips = [[i, i + 1] for i in range(0, rows, 2)]
    far_rows = trade(far, "gx", 1)
    near_rows = lax.all_gather(near, "gx", axis_index_groups=chips)
    (columns,) = local(close_columns, [(2 * GROUP, depth * 8)])(
        first, second, from_first, from_second, near_rows
    )
    far_columns = trade(columns, "gx", 1)
    near_columns = lax.all_gather(columns, "gx", axis_index_groups=chips)
    (halo,) = local(widen, [(depth * 8, 768)])(columns)
    sent, basis, pots = local(
        moments,
        [(rows, 128), (3, 2, depth, 16, 256), (2, depth, 16, 256)],
        [
            scratch(1, depth, 16, 256),
            scratch(4, depth, 16, 256),
            scratch(2, depth, 16, 256),
            scratch(2, depth * 8, 768),
        ],
    )(field, halo, near_rows, far_rows, near_columns, far_columns)
    received = lax.all_to_all(sent, "gx", 0, 0, tiled=True)
    (sent,) = local(relay, [(cols, 128)])(received)
    received = lax.all_to_all(sent, "gy", 0, 0, tiled=True)
    adjoint, gradient = local(
        finish,
        [cotangent.shape, conductance.shape],
        [scratch(2, depth, 16, 256)],
        kind=jax.ShapeDtypeStruct,
    )(received, basis, pots)
    return adjoint, gradient


def solution(mesh):
    return jax.shard_map(
        per_device,
        mesh=mesh,
        in_specs=(
            P(None, "gx", "gy"),
            P(None, "gx", "gy"),
            P(None, None, "gx", "gy"),
            P(None, None, "gx", "gy"),
        ),
        out_specs=(P(None, None, "gx", "gy"), P(None, "gx", "gy")),
        check_vma=False,
    )
```

```python
import jax
import jax.numpy as jnp
from jax import lax
from jax.experimental import pallas as pl
from jax.experimental.pallas import tpu as pltpu
from jax.sharding import PartitionSpec as P

SHIFT = 2.0
SPAN = 32.0
STEP_LOW = 1.0 / 61.0
SECOND = 64
COND, MASK, RES1, RES2, POT1, POT2 = range(6)
WIDTH = (3, 2, 3, 3, 1, 1)
LANE = (0, 9, 3, 6, 11, 12)
SLOT = (0, 6, 3, 8, 11, 12)
GROUP = 16


def roll(x, amount, axis):
    amount = amount % x.shape[axis]
    return x if amount == 0 else pltpu.roll(x, amount, axis)


def fields_at(cond, labels, cot, saved, z):
    tag = labels[z]
    free = tag == 0
    mask = jnp.where(free, 1.0, 0.0)
    pots = [jnp.where(tag == k + 1, 1.0, jnp.where(free, saved[k, z], 0.0)) for k in range(2)]
    return [cond[z], mask] + [jnp.where(free, cot[k, z], 0.0) for k in range(2)] + pots


def lanes_of(shape=(8, 128)):
    return lax.broadcasted_iota(jnp.int32, shape, 1)


def within(index, low, count):
    return (index >= low) & (index < low + count)


def exact_dot(x, matrix):
    total = None
    for _ in range(3):
        term = x.astype(jnp.bfloat16)
        x = x - term.astype(jnp.float32)
        part = jnp.dot(term, matrix, preferred_element_type=jnp.float32)
        total = part if total is None else total + part
    return total


def difference_matrices():
    i = lax.broadcasted_iota(jnp.int32, (256, 256), 0)
    j = lax.broadcasted_iota(jnp.int32, (256, 256), 1)
    here = jnp.where(i == j, 1.0, 0.0)
    forward = here - jnp.where(i == (j + 1) % 256, 1.0, 0.0)
    backward = here - jnp.where((i + 1) % 256 == j, 1.0, 0.0)
    return forward.astype(jnp.bfloat16), backward.astype(jnp.bfloat16)


def place(shape, rows, cols, pairs):
    i = lax.broadcasted_iota(jnp.int32, shape, rows)
    j = lax.broadcasted_iota(jnp.int32, shape, cols)
    hit = i < 0
    for row, col, count in pairs:
        hit |= within(i, row, count) & (j - i == col - row)
    return jnp.where(hit, 1.0, 0.0).astype(jnp.bfloat16)


def pack_columns(cond_in, labels_in, cot_in, saved_in, first, second, field, cond, labels, cot, saved, sems):
    copies = [
        pltpu.make_async_copy(source, target, sems.at[i])
        for i, (source, target) in enumerate(
            ((cond_in, cond), (labels_in, labels), (cot_in, cot), (saved_in, saved))
        )
    ]
    for copy in copies:
        copy.start()
    picks = [
        place(
            (128, 128),
            0,
            1,
            [(0, LANE[f], WIDTH[f]), (128 - WIDTH[f], GROUP + LANE[f], WIDTH[f])],
        )
        for f in range(6)
    ]
    for copy in copies:
        copy.wait()
    even = lax.axis_index("gy") % 2 == 0
    depth = cond.shape[0]
    for z in range(depth):
        for f, x in enumerate(fields_at(cond, labels, cot, saved, z)):
            field[f, z] = x
    total = None
    for f in range(6):
        part = exact_dot(field[f].reshape(depth * 8, 128), picks[f])
        total = part if total is None else total + part
    columns = total.T
    left, right = columns[0:GROUP], columns[GROUP : 2 * GROUP]
    first[...] = jnp.where(even, right, left)
    second[...] = jnp.where(even, left, right)


def unpack_columns(left, right, out):
    packed = jnp.concatenate([left, right], axis=0).T
    for f in range(6):
        w = WIDTH[f]
        matrix = place(
            (2 * GROUP, 128), 0, 1, [(LANE[f], 128 - w, w), (GROUP + LANE[f], 0, w)]
        )
        out[:, f * 128 : (f + 1) * 128] = exact_dot(packed, matrix)


def hold(source, target):
    target[...] = source[...]


def widen(field, sent_first, sent_second, from_second, from_first, wide, near, far, halo):
    even = lax.axis_index("gy") % 2 == 0
    upper = lax.axis_index("gx") % 2 == 0
    depth = field.shape[1]
    slot = lax.broadcasted_iota(jnp.int32, (GROUP, 128), 0)
    c = LANE[COND]

    def choose(a, b):
        return jnp.where(even, a[...], b[...])

    left, right = choose(from_second, from_first), choose(from_first, from_second)
    own_left, own_right = choose(sent_second, sent_first), choose(sent_first, sent_second)
    pot = (slot == LANE[POT1]) | (slot == LANE[POT2])
    outside = right[c : c + 1] == 0.0
    right = jnp.where(outside & (slot == c), -roll(own_right, -2, 0), right)
    right = jnp.where(outside & pot, own_right, right)
    outside = left[c + 2 : c + 3] == 0.0
    left = jnp.where(outside & (slot == c + 2), -roll(own_left, 2, 0), left)
    left = jnp.where(outside & pot, own_left, left)
    near[depth] = left
    near[depth + 1] = right
    far[depth] = left
    far[depth + 1] = right
    unpack_columns(left, right, halo)
    for z in range(depth):
        fields = [field[f, z] for f in range(6)]
        for f in range(6):
            wide[f, z, :, 0:128] = fields[f]
            wide[f, z, :, 128:256] = halo[8 * z : 8 * z + 8, f * 128 : (f + 1) * 128]
        own = []
        for side in range(2):
            rows = []
            for f in (COND, RES1, MASK, RES2, POT1, POT2):
                w = WIDTH[f]
                start = 0 if side == 0 else 8 - w
                rows.append(fields[f][start : start + w])
            own.append(jnp.concatenate(rows + [jnp.zeros((3, 128), jnp.float32)], axis=0))
        near[z] = jnp.where(upper, own[1], own[0])
        far[z] = jnp.where(upper, own[0], own[1])


def moments(wide, from_near, from_far, sent, basis, pots, field, weight, flux, corner):
    depth = wide.shape[1]
    core = lax.axis_index("gx") % 2
    lane16 = lanes_of((16, 128))
    row8 = lax.broadcasted_iota(jnp.int32, (8, 256), 0)

    def above(i):
        return jnp.where(core == 0, from_far[i], from_near[1 - core, i])

    def below(i):
        return jnp.where(core == 0, from_near[1 - core, i], from_far[i])

    for side, source in enumerate((above, below)):
        unpack_columns(source(depth), source(depth + 1), corner.at[side])
    for z in range(depth):
        top, bottom = above(z), below(z)
        parts = []
        for f in range(6):
            w, s = WIDTH[f], SLOT[f]
            own = wide[f, z]
            gap = jnp.zeros((8 - 2 * w, 128), jnp.float32)
            low = jnp.concatenate([bottom[s : s + w], gap, top[s : s + w]], axis=0)
            tips = [
                corner[side, 8 * z : 8 * z + 8, f * 128 : (f + 1) * 128] for side in range(2)
            ]
            high = jnp.concatenate([tips[1][0:w], gap, tips[0][8 - w : 8]], axis=0)
            parts.append((own, jnp.concatenate([low, high], axis=1)))
        own, other = parts[COND]
        outside = (other == 0.0) & ((row8 == 0) | (row8 == 7))

        def edge_value(x):
            return jnp.where(row8 == 0, roll(x, 1, 0), roll(x, -1, 0))

        parts[COND] = (own, jnp.where(outside, -edge_value(own), other))
        for f in (POT1, POT2):
            own, other = parts[f]
            parts[f] = (own, jnp.where(outside, edge_value(own), other))
        field[0, z, 0:8], field[0, z, 8:16] = parts[COND]
        weight[3, z, 0:8] = parts[MASK][0] * (1.0 / SPAN)
        weight[3, z, 8:16] = parts[MASK][1] * (1.0 / SPAN)
        for k in range(2):
            basis[0, k, z, 0:8], basis[0, k, z, 8:16] = parts[RES1 + k]
            pots[k, z, 0:8], pots[k, z, 8:16] = parts[POT1 + k]
    for z in range(depth):
        c = field[0, z]
        weight[0, z] = 0.5 * (c + roll(c, -1, 0))
        weight[1, z] = 0.5 * (c + roll(c, -1, 1))
        if z + 1 < depth:
            weight[2, z] = 0.5 * (c + field[0, z + 1])

    forward, backward = difference_matrices()

    def image(k, z, source, carry):
        u = basis[source, k, z]
        fx = weight[0, z] * (u - roll(u, -1, 0))
        total = (fx - roll(fx, 1, 0)) + flux[k, z] - u
        if carry is not None:
            total = total - carry
        carry = None
        if z + 1 < depth:
            carry = weight[2, z] * (u - basis[source, k, z + 1])
            total = total + carry
        return weight[3, z] * total, carry

    def lane_fluxes(source, rows):
        for k in range(2):
            u = basis[source, k, :, 0:rows].reshape(depth * rows, 256)
            f = weight[1, :, 0:rows].reshape(depth * rows, 256) * exact_dot(u, forward)
            flux[k, :, 0:rows] = exact_dot(f, backward).reshape(depth, rows, 256)

    for power in range(2):
        lane_fluxes(power, 16)
        for k in range(2):
            carry = None
            for z in range(depth):
                value, carry = image(k, z, power, carry)
                basis[power + 1, k, z] = value
    own = (slice(0, 8), slice(0, 128))

    def own_image(k, z, carry):
        u = basis[2, k, z, :, 0:128]
        fx = weight[0, z, :, 0:128] * (u - roll(u, -1, 0))
        u = u[0:8]
        total = (fx - roll(fx, 1, 0))[0:8] + flux[k, z, 0:8, 0:128] - u
        if carry is not None:
            total = total - carry
        carry = None
        if z + 1 < depth:
            carry = weight[2, z, 0:8, 0:128] * (u - basis[2, k, z + 1, 0:8, 0:128])
            total = total + carry
        return weight[3, z, 0:8, 0:128] * total, carry

    lane_fluxes(2, 8)
    totals = []
    for k in range(2):
        sums = [jnp.zeros((8, 128), jnp.float32) for _ in range(6)]
        carry = None
        for z in range(depth):
            last, carry = own_image(k, z, carry)
            v = [basis[i, k, z, 0:8, 0:128] for i in range(3)] + [last]
            sums = [s + v[i // 2] * v[i - i // 2] for i, s in enumerate(sums)]
        totals += sums
    sub = lax.broadcasted_iota(jnp.int32, (16, 128), 0)
    packed = jnp.zeros((16, 128), jnp.float32)
    for i, s in enumerate(totals):
        packed = jnp.where(sub == i, jnp.sum(s, axis=0, keepdims=True), packed)
    packed = jnp.sum(packed, axis=1, keepdims=True)
    target = jnp.where(sub < 6, sub, sub - 6 + SECOND)
    row = jnp.sum(jnp.where((lane16 == target) & (sub < 12), packed, 0.0), axis=0, keepdims=True)
    sent[...] = jnp.broadcast_to(row, sent.shape)


def relay(received, sent):
    sent[...] = jnp.broadcast_to(jnp.sum(received[...], axis=0, keepdims=True), sent.shape)


def coefficients(nu):
    def inner(a, b, lift):
        total = None
        for i, x in enumerate(a):
            for j, y in enumerate(b):
                term = (x * y) * nu[i + j + lift]
                total = term if total is None else total + term
        return total

    residual = [jnp.ones_like(nu[0])]
    direction = residual
    answer = []
    norm = nu[0]
    for iteration in range(3):
        energy = SHIFT * inner(direction, direction, 0) + SPAN * inner(direction, direction, 1)
        step = jnp.clip(norm / energy, STEP_LOW, 1.0)
        answer = [a + step * d for a, d in zip(answer + [0.0], direction)]
        if iteration == 2:
            return answer
        image = [SHIFT * d for d in direction] + [0.0]
        image = [i + SPAN * d for i, d in zip(image, [0.0] + direction)]
        residual = [r - step * i for r, i in zip(residual + [0.0], image)]
        new = jnp.maximum(inner(residual, residual, 0), 0.0)
        ratio = new / norm
        direction = [r + ratio * d for r, d in zip(residual, direction + [0.0])]
        norm = new


def finish(received, basis, pots, adjoint, gradient, field):
    depth = basis.shape[2]
    row = jnp.sum(received[...], axis=0, keepdims=True)
    row = jnp.broadcast_to(row, (8, 128))
    combined = coefficients([roll(row, -i, 1) for i in range(6)])
    lane = lanes_of()
    scale = [
        [
            jnp.sum(jnp.where(lane == k * SECOND, c, 0.0), axis=1, keepdims=True)[0:1, 0:1]
            for c in combined
        ]
        for k in range(2)
    ]
    for k in range(2):
        c = [jnp.broadcast_to(x, (16, 256)) for x in scale[k]]
        for z in range(depth):
            value = c[0] * basis[0, k, z] + c[1] * basis[1, k, z] + c[2] * basis[2, k, z]
            field[k, z] = value
            adjoint[k, z] = value[0:8, 0:128]
    carry = None
    for z in range(depth):
        gx = gy = gz = None
        for k in range(2):
            a, p = field[k, z], pots[k, z]
            tx = (a - roll(a, -1, 0)) * (p - roll(p, -1, 0))
            ty = (a - roll(a, -1, 1)) * (p - roll(p, -1, 1))
            gx = tx if gx is None else gx + tx
            gy = ty if gy is None else gy + ty
            if z + 1 < depth:
                tz = (a[0:8, 0:128] - field[k, z + 1, 0:8, 0:128]) * (
                    p[0:8, 0:128] - pots[k, z + 1, 0:8, 0:128]
                )
                gz = tz if gz is None else gz + tz
        total = (gx + roll(gx, 1, 0) + gy + roll(gy, 1, 1))[0:8, 0:128]
        if carry is not None:
            total = total + carry
        if gz is not None:
            total = total + gz
        carry = gz
        gradient[z] = -0.5 * total


def local(body, outs, scratch=(), space=pltpu.VMEM, limit=32 * 2**20, kind=pltpu.VMEM):
    vmem = pl.BlockSpec(memory_space=pltpu.VMEM)
    shapes = [kind(s, jnp.float32) for s in outs]

    def call(*args):
        return pl.pallas_call(
            body,
            out_shape=shapes,
            in_specs=[pl.BlockSpec(memory_space=space)] * len(args),
            out_specs=[vmem] * len(outs),
            scratch_shapes=list(scratch),
            compiler_params=pltpu.CompilerParams(vmem_limit_bytes=limit),
        )(*args)

    return call


def scratch(*shape, dtype=jnp.float32):
    return pltpu.VMEM(shape, dtype)


def trade(x, axis, start):
    pairs = [(i, i + 1) for i in range(start, lax.axis_size(axis) - 1, 2)]
    return lax.ppermute(x, axis, pairs + [(j, i) for i, j in pairs])


def per_device(conductance, labels, cotangent, saved):
    depth = conductance.shape[0]
    rows, cols = lax.axis_size("gx"), lax.axis_size("gy")
    args = (conductance, labels, cotangent, saved)
    first, second, field = local(
        pack_columns,
        [(GROUP, depth * 8)] * 2 + [(6, depth, 8, 128)],
        [scratch(*x.shape, dtype=x.dtype) for x in args] + [pltpu.SemaphoreType.DMA((4,))],
        pltpu.HBM,
        56 * 2**20,
    )(*args)
    from_second = trade(second, "gy", 1)
    (from_second,) = local(hold, [(GROUP, depth * 8)])(from_second)
    from_first = trade(first, "gy", 0)
    wide, near, far = local(
        widen,
        [(6, depth, 8, 256)] + [(depth + 2, 16, 128)] * 2,
        [scratch(depth * 8, 768)],
    )(field, first, second, from_second, from_first)
    far = trade(far, "gx", 1)
    near = lax.all_gather(near, "gx", axis_index_groups=[[i, i + 1] for i in range(0, rows, 2)])
    sent, basis, pots = local(
        moments,
        [(rows, 128), (3, 2, depth, 16, 256), (2, depth, 16, 256)],
        [scratch(1, depth, 16, 256), scratch(4, depth, 16, 256), scratch(2, depth, 16, 256), scratch(2, depth * 8, 768)],
    )(wide, near, far)
    received = lax.all_to_all(sent, "gx", 0, 0, tiled=True)
    (sent,) = local(relay, [(cols, 128)])(received)
    received = lax.all_to_all(sent, "gy", 0, 0, tiled=True)
    adjoint, gradient = local(
        finish,
        [cotangent.shape, conductance.shape],
        [scratch(2, depth, 16, 256)],
        kind=jax.ShapeDtypeStruct,
    )(received, basis, pots)
    return adjoint, gradient


def solution(mesh):
    return jax.shard_map(
        per_device,
        mesh=mesh,
        in_specs=(
            P(None, "gx", "gy"),
            P(None, "gx", "gy"),
            P(None, None, "gx", "gy"),
            P(None, None, "gx", "gy"),
        ),
        out_specs=(P(None, None, "gx", "gy"), P(None, "gx", "gy")),
        check_vma=False,
    )
```

```python
import jax
import jax.numpy as jnp
from jax import lax
from jax.experimental import pallas as pl
from jax.experimental.pallas import tpu as pltpu
from jax.sharding import PartitionSpec as P

SHIFT = 2.0
SPAN = 32.0
STEP_LOW = 1.0 / 61.0
SECOND = 64
COND, MASK, RES1, RES2, POT1, POT2 = range(6)
WIDTH = (3, 2, 3, 3, 1, 1)
LANE = (0, 9, 3, 6, 11, 12)
SLOT = (0, 6, 3, 8, 11, 12)
GROUP = 16
ROWS = sum(WIDTH)


def roll(x, amount, axis):
    amount = amount % x.shape[axis]
    return x if amount == 0 else pltpu.roll(x, amount, axis)


def fields_at(cond, labels, cot, saved, z):
    tag = labels[z]
    free = tag == 0
    mask = jnp.where(free, 1.0, 0.0)
    pots = [jnp.where(tag == k + 1, 1.0, jnp.where(free, saved[k, z], 0.0)) for k in range(2)]
    return [cond[z], mask] + [jnp.where(free, cot[k, z], 0.0) for k in range(2)] + pots


def lanes_of(shape=(8, 128)):
    return lax.broadcasted_iota(jnp.int32, shape, 1)


def within(index, low, count):
    return (index >= low) & (index < low + count)


def exact_dot(x, matrix):
    total = None
    for _ in range(3):
        term = x.astype(jnp.bfloat16)
        x = x - term.astype(jnp.float32)
        part = jnp.dot(term, matrix, preferred_element_type=jnp.float32)
        total = part if total is None else total + part
    return total


def difference_matrices():
    i = lax.broadcasted_iota(jnp.int32, (256, 256), 0)
    j = lax.broadcasted_iota(jnp.int32, (256, 256), 1)
    here = jnp.where(i == j, 1.0, 0.0)
    forward = here - jnp.where(i == (j + 1) % 256, 1.0, 0.0)
    backward = here - jnp.where((i + 1) % 256 == j, 1.0, 0.0)
    return forward.astype(jnp.bfloat16), backward.astype(jnp.bfloat16)


def place(shape, rows, cols, pairs):
    i = lax.broadcasted_iota(jnp.int32, shape, rows)
    j = lax.broadcasted_iota(jnp.int32, shape, cols)
    hit = i < 0
    for row, col, count in pairs:
        hit |= within(i, row, count) & (j - i == col - row)
    return jnp.where(hit, 1.0, 0.0).astype(jnp.bfloat16)


def pack_columns(cond_in, labels_in, cot_in, saved_in, first, second, field, cond, labels, cot, saved, sems):
    copies = [
        pltpu.make_async_copy(source, target, sems.at[i])
        for i, (source, target) in enumerate(
            ((cond_in, cond), (labels_in, labels), (cot_in, cot), (saved_in, saved))
        )
    ]
    for copy in copies:
        copy.start()
    picks = [
        place(
            (128, 128),
            0,
            1,
            [(0, LANE[f], WIDTH[f]), (128 - WIDTH[f], GROUP + LANE[f], WIDTH[f])],
        )
        for f in range(6)
    ]
    for copy in copies:
        copy.wait()
    even = lax.axis_index("gy") % 2 == 0
    depth = cond.shape[0]
    for z in range(depth):
        for f, x in enumerate(fields_at(cond, labels, cot, saved, z)):
            field[f, z] = x
    total = None
    for f in range(6):
        part = exact_dot(field[f].reshape(depth * 8, 128), picks[f])
        total = part if total is None else total + part
    columns = total.T
    left, right = columns[0:GROUP], columns[GROUP : 2 * GROUP]
    first[...] = jnp.where(even, right, left)
    second[...] = jnp.where(even, left, right)


def unpack_columns(left, right, out):
    packed = jnp.concatenate([left, right], axis=0).T
    for f in range(6):
        w = WIDTH[f]
        matrix = place(
            (2 * GROUP, 128), 0, 1, [(LANE[f], 128 - w, w), (GROUP + LANE[f], 0, w)]
        )
        out[:, f * 128 : (f + 1) * 128] = exact_dot(packed, matrix)


def hold(source, target):
    target[...] = source[...]


def widen(field, sent_first, sent_second, from_second, from_first, wide, near, far, halo):
    even = lax.axis_index("gy") % 2 == 0
    upper = lax.axis_index("gx") % 2 == 0
    depth = field.shape[1]
    slot = lax.broadcasted_iota(jnp.int32, (GROUP, 128), 0)
    c = LANE[COND]

    def choose(a, b):
        return jnp.where(even, a[...], b[...])

    left, right = choose(from_second, from_first), choose(from_first, from_second)
    own_left, own_right = choose(sent_second, sent_first), choose(sent_first, sent_second)
    pot = (slot == LANE[POT1]) | (slot == LANE[POT2])
    outside = right[c : c + 1] == 0.0
    right = jnp.where(outside & (slot == c), -roll(own_right, -2, 0), right)
    right = jnp.where(outside & pot, own_right, right)
    outside = left[c + 2 : c + 3] == 0.0
    left = jnp.where(outside & (slot == c + 2), -roll(own_left, 2, 0), left)
    left = jnp.where(outside & pot, own_left, left)
    columns = jnp.concatenate([left[0:ROWS], right[0:ROWS]], axis=0)
    start, end = ROWS * depth, ROWS * (depth + 2)
    for out in (near, far):
        out[start:end] = columns
        if out.shape[0] > end:
            out[end:] = jnp.zeros((out.shape[0] - end, 128), jnp.float32)
    unpack_columns(left, right, halo)
    for z in range(depth):
        fields = [field[f, z] for f in range(6)]
        for f in range(6):
            wide[f, z, :, 0:128] = fields[f]
            wide[f, z, :, 128:256] = halo[8 * z : 8 * z + 8, f * 128 : (f + 1) * 128]
        own = []
        for side in range(2):
            rows = []
            for f in (COND, RES1, MASK, RES2, POT1, POT2):
                w = WIDTH[f]
                start = 0 if side == 0 else 8 - w
                rows.append(fields[f][start : start + w])
            own.append(jnp.concatenate(rows, axis=0))
        near[ROWS * z : ROWS * (z + 1)] = jnp.where(upper, own[1], own[0])
        far[ROWS * z : ROWS * (z + 1)] = jnp.where(upper, own[0], own[1])


def moments(wide, from_near, from_far, sent, basis, pots, field, weight, flux, corner):
    depth = wide.shape[1]
    core = lax.axis_index("gx") % 2
    lane16 = lanes_of((16, 128))
    row8 = lax.broadcasted_iota(jnp.int32, (8, 256), 0)

    def above(i):
        rows = slice(ROWS * i, ROWS * (i + 1))
        return jnp.where(core == 0, from_far[rows], from_near[1 - core, rows])

    def below(i):
        rows = slice(ROWS * i, ROWS * (i + 1))
        return jnp.where(core == 0, from_near[1 - core, rows], from_far[rows])

    blank = jnp.zeros((GROUP - ROWS, 128), jnp.float32)
    for side, source in enumerate((above, below)):
        tips = [jnp.concatenate([source(depth + i), blank], axis=0) for i in range(2)]
        unpack_columns(*tips, corner.at[side])
    for z in range(depth):
        top, bottom = above(z), below(z)
        parts = []
        for f in range(6):
            w, s = WIDTH[f], SLOT[f]
            own = wide[f, z]
            gap = jnp.zeros((8 - 2 * w, 128), jnp.float32)
            low = jnp.concatenate([bottom[s : s + w], gap, top[s : s + w]], axis=0)
            tips = [
                corner[side, 8 * z : 8 * z + 8, f * 128 : (f + 1) * 128] for side in range(2)
            ]
            high = jnp.concatenate([tips[1][0:w], gap, tips[0][8 - w : 8]], axis=0)
            parts.append((own, jnp.concatenate([low, high], axis=1)))
        own, other = parts[COND]
        outside = (other == 0.0) & ((row8 == 0) | (row8 == 7))

        def edge_value(x):
            return jnp.where(row8 == 0, roll(x, 1, 0), roll(x, -1, 0))

        parts[COND] = (own, jnp.where(outside, -edge_value(own), other))
        for f in (POT1, POT2):
            own, other = parts[f]
            parts[f] = (own, jnp.where(outside, edge_value(own), other))
        field[0, z, 0:8], field[0, z, 8:16] = parts[COND]
        weight[3, z, 0:8] = parts[MASK][0] * (1.0 / SPAN)
        weight[3, z, 8:16] = parts[MASK][1] * (1.0 / SPAN)
        for k in range(2):
            basis[0, k, z, 0:8], basis[0, k, z, 8:16] = parts[RES1 + k]
            pots[k, z, 0:8], pots[k, z, 8:16] = parts[POT1 + k]
    for z in range(depth):
        c = field[0, z]
        weight[0, z] = 0.5 * (c + roll(c, -1, 0))
        weight[1, z] = 0.5 * (c + roll(c, -1, 1))
        if z + 1 < depth:
            weight[2, z] = 0.5 * (c + field[0, z + 1])

    forward, backward = difference_matrices()

    def image(k, z, source, carry):
        u = basis[source, k, z]
        fx = weight[0, z] * (u - roll(u, -1, 0))
        total = (fx - roll(fx, 1, 0)) + flux[k, z] - u
        if carry is not None:
            total = total - carry
        carry = None
        if z + 1 < depth:
            carry = weight[2, z] * (u - basis[source, k, z + 1])
            total = total + carry
        return weight[3, z] * total, carry

    def lane_fluxes(source, rows):
        for k in range(2):
            u = basis[source, k, :, 0:rows].reshape(depth * rows, 256)
            f = weight[1, :, 0:rows].reshape(depth * rows, 256) * exact_dot(u, forward)
            flux[k, :, 0:rows] = exact_dot(f, backward).reshape(depth, rows, 256)

    for power in range(2):
        lane_fluxes(power, 16)
        for k in range(2):
            carry = None
            for z in range(depth):
                value, carry = image(k, z, power, carry)
                basis[power + 1, k, z] = value
    own = (slice(0, 8), slice(0, 128))

    def own_image(k, z, carry):
        u = basis[2, k, z, :, 0:128]
        fx = weight[0, z, :, 0:128] * (u - roll(u, -1, 0))
        u = u[0:8]
        total = (fx - roll(fx, 1, 0))[0:8] + flux[k, z, 0:8, 0:128] - u
        if carry is not None:
            total = total - carry
        carry = None
        if z + 1 < depth:
            carry = weight[2, z, 0:8, 0:128] * (u - basis[2, k, z + 1, 0:8, 0:128])
            total = total + carry
        return weight[3, z, 0:8, 0:128] * total, carry

    lane_fluxes(2, 8)
    totals = []
    for k in range(2):
        sums = [jnp.zeros((8, 128), jnp.float32) for _ in range(6)]
        carry = None
        for z in range(depth):
            last, carry = own_image(k, z, carry)
            v = [basis[i, k, z, 0:8, 0:128] for i in range(3)] + [last]
            sums = [s + v[i // 2] * v[i - i // 2] for i, s in enumerate(sums)]
        totals += sums
    sub = lax.broadcasted_iota(jnp.int32, (16, 128), 0)
    packed = jnp.zeros((16, 128), jnp.float32)
    for i, s in enumerate(totals):
        packed = jnp.where(sub == i, jnp.sum(s, axis=0, keepdims=True), packed)
    packed = jnp.sum(packed, axis=1, keepdims=True)
    target = jnp.where(sub < 6, sub, sub - 6 + SECOND)
    row = jnp.sum(jnp.where((lane16 == target) & (sub < 12), packed, 0.0), axis=0, keepdims=True)
    sent[...] = jnp.broadcast_to(row, sent.shape)


def relay(received, sent):
    sent[...] = jnp.broadcast_to(jnp.sum(received[...], axis=0, keepdims=True), sent.shape)


def coefficients(nu):
    def inner(a, b, lift):
        total = None
        for i, x in enumerate(a):
            for j, y in enumerate(b):
                term = (x * y) * nu[i + j + lift]
                total = term if total is None else total + term
        return total

    residual = [jnp.ones_like(nu[0])]
    direction = residual
    answer = []
    norm = nu[0]
    for iteration in range(3):
        energy = SHIFT * inner(direction, direction, 0) + SPAN * inner(direction, direction, 1)
        step = jnp.clip(norm / energy, STEP_LOW, 1.0)
        answer = [a + step * d for a, d in zip(answer + [0.0], direction)]
        if iteration == 2:
            return answer
        image = [SHIFT * d for d in direction] + [0.0]
        image = [i + SPAN * d for i, d in zip(image, [0.0] + direction)]
        residual = [r - step * i for r, i in zip(residual + [0.0], image)]
        new = jnp.maximum(inner(residual, residual, 0), 0.0)
        ratio = new / norm
        direction = [r + ratio * d for r, d in zip(residual, direction + [0.0])]
        norm = new


def finish(received, basis, pots, adjoint, gradient, field):
    depth = basis.shape[2]
    row = jnp.sum(received[...], axis=0, keepdims=True)
    row = jnp.broadcast_to(row, (8, 128))
    combined = coefficients([roll(row, -i, 1) for i in range(6)])
    lane = lanes_of()
    scale = [
        [
            jnp.sum(jnp.where(lane == k * SECOND, c, 0.0), axis=1, keepdims=True)[0:1, 0:1]
            for c in combined
        ]
        for k in range(2)
    ]
    for k in range(2):
        c = [jnp.broadcast_to(x, (16, 256)) for x in scale[k]]
        for z in range(depth):
            value = c[0] * basis[0, k, z] + c[1] * basis[1, k, z] + c[2] * basis[2, k, z]
            field[k, z] = value
            adjoint[k, z] = value[0:8, 0:128]
    carry = None
    for z in range(depth):
        gx = gy = gz = None
        for k in range(2):
            a, p = field[k, z], pots[k, z]
            tx = (a - roll(a, -1, 0)) * (p - roll(p, -1, 0))
            ty = (a - roll(a, -1, 1)) * (p - roll(p, -1, 1))
            gx = tx if gx is None else gx + tx
            gy = ty if gy is None else gy + ty
            if z + 1 < depth:
                tz = (a[0:8, 0:128] - field[k, z + 1, 0:8, 0:128]) * (
                    p[0:8, 0:128] - pots[k, z + 1, 0:8, 0:128]
                )
                gz = tz if gz is None else gz + tz
        total = (gx + roll(gx, 1, 0) + gy + roll(gy, 1, 1))[0:8, 0:128]
        if carry is not None:
            total = total + carry
        if gz is not None:
            total = total + gz
        carry = gz
        gradient[z] = -0.5 * total


def local(body, outs, scratch=(), space=pltpu.VMEM, limit=32 * 2**20, kind=pltpu.VMEM):
    vmem = pl.BlockSpec(memory_space=pltpu.VMEM)
    shapes = [kind(s, jnp.float32) for s in outs]

    def call(*args):
        return pl.pallas_call(
            body,
            out_shape=shapes,
            in_specs=[pl.BlockSpec(memory_space=space)] * len(args),
            out_specs=[vmem] * len(outs),
            scratch_shapes=list(scratch),
            compiler_params=pltpu.CompilerParams(vmem_limit_bytes=limit),
        )(*args)

    return call


def scratch(*shape, dtype=jnp.float32):
    return pltpu.VMEM(shape, dtype)


def trade(x, axis, start):
    pairs = [(i, i + 1) for i in range(start, lax.axis_size(axis) - 1, 2)]
    return lax.ppermute(x, axis, pairs + [(j, i) for i, j in pairs])


def per_device(conductance, labels, cotangent, saved):
    depth = conductance.shape[0]
    rows, cols = lax.axis_size("gx"), lax.axis_size("gy")
    args = (conductance, labels, cotangent, saved)
    first, second, field = local(
        pack_columns,
        [(GROUP, depth * 8)] * 2 + [(6, depth, 8, 128)],
        [scratch(*x.shape, dtype=x.dtype) for x in args] + [pltpu.SemaphoreType.DMA((4,))],
        pltpu.HBM,
        56 * 2**20,
    )(*args)
    from_second = trade(second, "gy", 1)
    (from_second,) = local(hold, [(GROUP, depth * 8)])(from_second)
    from_first = trade(first, "gy", 0)
    wide, near, far = local(
        widen,
        [(6, depth, 8, 256)] + [(-(-ROWS * (depth + 2) // 8) * 8, 128)] * 2,
        [scratch(depth * 8, 768)],
    )(field, first, second, from_second, from_first)
    far = trade(far, "gx", 1)
    near = lax.all_gather(near, "gx", axis_index_groups=[[i, i + 1] for i in range(0, rows, 2)])
    sent, basis, pots = local(
        moments,
        [(rows, 128), (3, 2, depth, 16, 256), (2, depth, 16, 256)],
        [scratch(1, depth, 16, 256), scratch(4, depth, 16, 256), scratch(2, depth, 16, 256), scratch(2, depth * 8, 768)],
    )(wide, near, far)
    received = lax.all_to_all(sent, "gx", 0, 0, tiled=True)
    (sent,) = local(relay, [(cols, 128)])(received)
    received = lax.all_to_all(sent, "gy", 0, 0, tiled=True)
    adjoint, gradient = local(
        finish,
        [cotangent.shape, conductance.shape],
        [scratch(2, depth, 16, 256)],
        kind=jax.ShapeDtypeStruct,
    )(received, basis, pots)
    return adjoint, gradient


def solution(mesh):
    return jax.shard_map(
        per_device,
        mesh=mesh,
        in_specs=(
            P(None, "gx", "gy"),
            P(None, "gx", "gy"),
            P(None, None, "gx", "gy"),
            P(None, None, "gx", "gy"),
        ),
        out_specs=(P(None, None, "gx", "gy"), P(None, "gx", "gy")),
        check_vma=False,
    )
```

```python
import jax
import jax.numpy as jnp
from jax import lax
from jax.experimental import pallas as pl
from jax.experimental.pallas import tpu as pltpu
from jax.sharding import PartitionSpec as P

SHIFT = 2.0
SPAN = 32.0
STEP_LOW = 1.0 / 61.0
SECOND = 64
COND, MASK, RES1, RES2, POT1, POT2 = range(6)
WIDTH = (3, 2, 3, 3, 1, 1)
LANE = (0, 9, 3, 6, 11, 12)
SLOT = (0, 6, 3, 8, 11, 12)
GROUP = 16
ROWS = sum(WIDTH)


def roll(x, amount, axis):
    amount = amount % x.shape[axis]
    return x if amount == 0 else pltpu.roll(x, amount, axis)


def fields_at(cond, labels, cot, saved, z):
    tag = labels[z]
    free = tag == 0
    mask = jnp.where(free, 1.0, 0.0)
    pots = [jnp.where(tag == k + 1, 1.0, jnp.where(free, saved[k, z], 0.0)) for k in range(2)]
    return [cond[z], mask] + [jnp.where(free, cot[k, z], 0.0) for k in range(2)] + pots


def lanes_of(shape=(8, 128)):
    return lax.broadcasted_iota(jnp.int32, shape, 1)


def within(index, low, count):
    return (index >= low) & (index < low + count)


def exact_dot(x, matrix):
    total = None
    for _ in range(3):
        term = x.astype(jnp.bfloat16)
        x = x - term.astype(jnp.float32)
        part = jnp.dot(term, matrix, preferred_element_type=jnp.float32)
        total = part if total is None else total + part
    return total


def difference_matrices():
    i = lax.broadcasted_iota(jnp.int32, (256, 256), 0)
    j = lax.broadcasted_iota(jnp.int32, (256, 256), 1)
    here = jnp.where(i == j, 1.0, 0.0)
    forward = here - jnp.where(i == (j + 1) % 256, 1.0, 0.0)
    backward = here - jnp.where((i + 1) % 256 == j, 1.0, 0.0)
    return forward.astype(jnp.bfloat16), backward.astype(jnp.bfloat16)


def place(shape, rows, cols, pairs):
    i = lax.broadcasted_iota(jnp.int32, shape, rows)
    j = lax.broadcasted_iota(jnp.int32, shape, cols)
    hit = i < 0
    for row, col, count in pairs:
        hit |= within(i, row, count) & (j - i == col - row)
    return jnp.where(hit, 1.0, 0.0).astype(jnp.bfloat16)


def pack_columns(cond_in, labels_in, cot_in, saved_in, first, second, field, cond, labels, cot, saved, sems):
    copies = [
        pltpu.make_async_copy(source, target, sems.at[i])
        for i, (source, target) in enumerate(
            ((cond_in, cond), (labels_in, labels), (cot_in, cot), (saved_in, saved))
        )
    ]
    for copy in copies:
        copy.start()
    picks = [
        place(
            (128, 128),
            0,
            1,
            [(0, LANE[f], WIDTH[f]), (128 - WIDTH[f], GROUP + LANE[f], WIDTH[f])],
        )
        for f in range(6)
    ]
    for copy in copies:
        copy.wait()
    even = lax.axis_index("gy") % 2 == 0
    depth = cond.shape[0]
    for z in range(depth):
        for f, x in enumerate(fields_at(cond, labels, cot, saved, z)):
            field[f, z] = x
    total = None
    for f in range(6):
        part = exact_dot(field[f].reshape(depth * 8, 128), picks[f])
        total = part if total is None else total + part
    columns = total.T
    left, right = columns[0:GROUP], columns[GROUP : 2 * GROUP]
    first[...] = jnp.where(even, right, left)
    second[...] = jnp.where(even, left, right)


def unpack_columns(left, right, out):
    packed = jnp.concatenate([left, right], axis=0).T
    for f in range(6):
        w = WIDTH[f]
        matrix = place(
            (2 * GROUP, 128), 0, 1, [(LANE[f], 128 - w, w), (GROUP + LANE[f], 0, w)]
        )
        out[:, f * 128 : (f + 1) * 128] = exact_dot(packed, matrix)


def hold(source, target):
    target[...] = source[...]


def pack_rows(field, sent_first, sent_second, from_second, from_first, near, far, closed):
    even = lax.axis_index("gy") % 2 == 0
    upper = lax.axis_index("gx") % 2 == 0
    depth = field.shape[1]
    slot = lax.broadcasted_iota(jnp.int32, (GROUP, 128), 0)
    c = LANE[COND]

    def choose(a, b):
        return jnp.where(even, a[...], b[...])

    left, right = choose(from_second, from_first), choose(from_first, from_second)
    own_left, own_right = choose(sent_second, sent_first), choose(sent_first, sent_second)
    pot = (slot == LANE[POT1]) | (slot == LANE[POT2])
    outside = right[c : c + 1] == 0.0
    right = jnp.where(outside & (slot == c), -roll(own_right, -2, 0), right)
    right = jnp.where(outside & pot, own_right, right)
    outside = left[c + 2 : c + 3] == 0.0
    left = jnp.where(outside & (slot == c + 2), -roll(own_left, 2, 0), left)
    left = jnp.where(outside & pot, own_left, left)
    columns = jnp.concatenate([left[0:ROWS], right[0:ROWS]], axis=0)
    start, end = ROWS * depth, ROWS * (depth + 2)
    for out in (near, far):
        out[start:end] = columns
        if out.shape[0] > end:
            out[end:] = jnp.zeros((out.shape[0] - end, 128), jnp.float32)
    closed[0] = left
    closed[1] = right
    for z in range(depth):
        fields = [field[f, z] for f in range(6)]
        own = []
        for side in range(2):
            rows = []
            for f in (COND, RES1, MASK, RES2, POT1, POT2):
                w = WIDTH[f]
                start = 0 if side == 0 else 8 - w
                rows.append(fields[f][start : start + w])
            own.append(jnp.concatenate(rows, axis=0))
        near[ROWS * z : ROWS * (z + 1)] = jnp.where(upper, own[1], own[0])
        far[ROWS * z : ROWS * (z + 1)] = jnp.where(upper, own[0], own[1])


def widen(field, closed, wide, halo):
    unpack_columns(closed[0], closed[1], halo)
    for z in range(field.shape[1]):
        for f in range(6):
            wide[f, z, :, 0:128] = field[f, z]
            wide[f, z, :, 128:256] = halo[8 * z : 8 * z + 8, f * 128 : (f + 1) * 128]


def moments(wide, from_near, from_far, sent, basis, pots, field, weight, flux, corner):
    depth = wide.shape[1]
    core = lax.axis_index("gx") % 2
    lane16 = lanes_of((16, 128))
    row8 = lax.broadcasted_iota(jnp.int32, (8, 256), 0)

    def above(i):
        rows = slice(ROWS * i, ROWS * (i + 1))
        return jnp.where(core == 0, from_far[rows], from_near[1 - core, rows])

    def below(i):
        rows = slice(ROWS * i, ROWS * (i + 1))
        return jnp.where(core == 0, from_near[1 - core, rows], from_far[rows])

    blank = jnp.zeros((GROUP - ROWS, 128), jnp.float32)
    for side, source in enumerate((above, below)):
        tips = [jnp.concatenate([source(depth + i), blank], axis=0) for i in range(2)]
        unpack_columns(*tips, corner.at[side])
    for z in range(depth):
        top, bottom = above(z), below(z)
        parts = []
        for f in range(6):
            w, s = WIDTH[f], SLOT[f]
            own = wide[f, z]
            gap = jnp.zeros((8 - 2 * w, 128), jnp.float32)
            low = jnp.concatenate([bottom[s : s + w], gap, top[s : s + w]], axis=0)
            tips = [
                corner[side, 8 * z : 8 * z + 8, f * 128 : (f + 1) * 128] for side in range(2)
            ]
            high = jnp.concatenate([tips[1][0:w], gap, tips[0][8 - w : 8]], axis=0)
            parts.append((own, jnp.concatenate([low, high], axis=1)))
        own, other = parts[COND]
        outside = (other == 0.0) & ((row8 == 0) | (row8 == 7))

        def edge_value(x):
            return jnp.where(row8 == 0, roll(x, 1, 0), roll(x, -1, 0))

        parts[COND] = (own, jnp.where(outside, -edge_value(own), other))
        for f in (POT1, POT2):
            own, other = parts[f]
            parts[f] = (own, jnp.where(outside, edge_value(own), other))
        field[0, z, 0:8], field[0, z, 8:16] = parts[COND]
        weight[3, z, 0:8] = parts[MASK][0] * (1.0 / SPAN)
        weight[3, z, 8:16] = parts[MASK][1] * (1.0 / SPAN)
        for k in range(2):
            basis[0, k, z, 0:8], basis[0, k, z, 8:16] = parts[RES1 + k]
            pots[k, z, 0:8], pots[k, z, 8:16] = parts[POT1 + k]
    for z in range(depth):
        c = field[0, z]
        weight[0, z] = 0.5 * (c + roll(c, -1, 0))
        weight[1, z] = 0.5 * (c + roll(c, -1, 1))
        if z + 1 < depth:
            weight[2, z] = 0.5 * (c + field[0, z + 1])

    forward, backward = difference_matrices()

    def image(k, z, source, carry):
        u = basis[source, k, z]
        fx = weight[0, z] * (u - roll(u, -1, 0))
        total = (fx - roll(fx, 1, 0)) + flux[k, z] - u
        if carry is not None:
            total = total - carry
        carry = None
        if z + 1 < depth:
            carry = weight[2, z] * (u - basis[source, k, z + 1])
            total = total + carry
        return weight[3, z] * total, carry

    def lane_fluxes(source, rows):
        for k in range(2):
            u = basis[source, k, :, 0:rows].reshape(depth * rows, 256)
            f = weight[1, :, 0:rows].reshape(depth * rows, 256) * exact_dot(u, forward)
            flux[k, :, 0:rows] = exact_dot(f, backward).reshape(depth, rows, 256)

    for power in range(2):
        lane_fluxes(power, 16)
        for k in range(2):
            carry = None
            for z in range(depth):
                value, carry = image(k, z, power, carry)
                basis[power + 1, k, z] = value
    own = (slice(0, 8), slice(0, 128))

    def own_image(k, z, carry):
        u = basis[2, k, z, :, 0:128]
        fx = weight[0, z, :, 0:128] * (u - roll(u, -1, 0))
        u = u[0:8]
        total = (fx - roll(fx, 1, 0))[0:8] + flux[k, z, 0:8, 0:128] - u
        if carry is not None:
            total = total - carry
        carry = None
        if z + 1 < depth:
            carry = weight[2, z, 0:8, 0:128] * (u - basis[2, k, z + 1, 0:8, 0:128])
            total = total + carry
        return weight[3, z, 0:8, 0:128] * total, carry

    lane_fluxes(2, 8)
    totals = []
    for k in range(2):
        sums = [jnp.zeros((8, 128), jnp.float32) for _ in range(6)]
        carry = None
        for z in range(depth):
            last, carry = own_image(k, z, carry)
            v = [basis[i, k, z, 0:8, 0:128] for i in range(3)] + [last]
            sums = [s + v[i // 2] * v[i - i // 2] for i, s in enumerate(sums)]
        totals += sums
    sub = lax.broadcasted_iota(jnp.int32, (16, 128), 0)
    packed = jnp.zeros((16, 128), jnp.float32)
    for i, s in enumerate(totals):
        packed = jnp.where(sub == i, jnp.sum(s, axis=0, keepdims=True), packed)
    packed = jnp.sum(packed, axis=1, keepdims=True)
    target = jnp.where(sub < 6, sub, sub - 6 + SECOND)
    row = jnp.sum(jnp.where((lane16 == target) & (sub < 12), packed, 0.0), axis=0, keepdims=True)
    sent[...] = jnp.broadcast_to(row, sent.shape)


def relay(received, sent):
    sent[...] = jnp.broadcast_to(jnp.sum(received[...], axis=0, keepdims=True), sent.shape)


def coefficients(nu):
    def inner(a, b, lift):
        total = None
        for i, x in enumerate(a):
            for j, y in enumerate(b):
                term = (x * y) * nu[i + j + lift]
                total = term if total is None else total + term
        return total

    residual = [jnp.ones_like(nu[0])]
    direction = residual
    answer = []
    norm = nu[0]
    for iteration in range(3):
        energy = SHIFT * inner(direction, direction, 0) + SPAN * inner(direction, direction, 1)
        step = jnp.clip(norm / energy, STEP_LOW, 1.0)
        answer = [a + step * d for a, d in zip(answer + [0.0], direction)]
        if iteration == 2:
            return answer
        image = [SHIFT * d for d in direction] + [0.0]
        image = [i + SPAN * d for i, d in zip(image, [0.0] + direction)]
        residual = [r - step * i for r, i in zip(residual + [0.0], image)]
        new = jnp.maximum(inner(residual, residual, 0), 0.0)
        ratio = new / norm
        direction = [r + ratio * d for r, d in zip(residual, direction + [0.0])]
        norm = new


def finish(received, basis, pots, adjoint, gradient, field):
    depth = basis.shape[2]
    row = jnp.sum(received[...], axis=0, keepdims=True)
    row = jnp.broadcast_to(row, (8, 128))
    combined = coefficients([roll(row, -i, 1) for i in range(6)])
    lane = lanes_of()
    scale = [
        [
            jnp.sum(jnp.where(lane == k * SECOND, c, 0.0), axis=1, keepdims=True)[0:1, 0:1]
            for c in combined
        ]
        for k in range(2)
    ]
    for k in range(2):
        c = [jnp.broadcast_to(x, (16, 256)) for x in scale[k]]
        for z in range(depth):
            value = c[0] * basis[0, k, z] + c[1] * basis[1, k, z] + c[2] * basis[2, k, z]
            field[k, z] = value
            adjoint[k, z] = value[0:8, 0:128]
    carry = None
    for z in range(depth):
        gx = gy = gz = None
        for k in range(2):
            a, p = field[k, z], pots[k, z]
            tx = (a - roll(a, -1, 0)) * (p - roll(p, -1, 0))
            ty = (a - roll(a, -1, 1)) * (p - roll(p, -1, 1))
            gx = tx if gx is None else gx + tx
            gy = ty if gy is None else gy + ty
            if z + 1 < depth:
                tz = (a[0:8, 0:128] - field[k, z + 1, 0:8, 0:128]) * (
                    p[0:8, 0:128] - pots[k, z + 1, 0:8, 0:128]
                )
                gz = tz if gz is None else gz + tz
        total = (gx + roll(gx, 1, 0) + gy + roll(gy, 1, 1))[0:8, 0:128]
        if carry is not None:
            total = total + carry
        if gz is not None:
            total = total + gz
        carry = gz
        gradient[z] = -0.5 * total


def local(body, outs, scratch=(), space=pltpu.VMEM, limit=32 * 2**20, kind=pltpu.VMEM):
    vmem = pl.BlockSpec(memory_space=pltpu.VMEM)
    shapes = [kind(s, jnp.float32) for s in outs]

    def call(*args):
        return pl.pallas_call(
            body,
            out_shape=shapes,
            in_specs=[pl.BlockSpec(memory_space=space)] * len(args),
            out_specs=[vmem] * len(outs),
            scratch_shapes=list(scratch),
            compiler_params=pltpu.CompilerParams(vmem_limit_bytes=limit),
        )(*args)

    return call


def scratch(*shape, dtype=jnp.float32):
    return pltpu.VMEM(shape, dtype)


def trade(x, axis, start):
    pairs = [(i, i + 1) for i in range(start, lax.axis_size(axis) - 1, 2)]
    return lax.ppermute(x, axis, pairs + [(j, i) for i, j in pairs])


def per_device(conductance, labels, cotangent, saved):
    depth = conductance.shape[0]
    rows, cols = lax.axis_size("gx"), lax.axis_size("gy")
    args = (conductance, labels, cotangent, saved)
    first, second, field = local(
        pack_columns,
        [(GROUP, depth * 8)] * 2 + [(6, depth, 8, 128)],
        [scratch(*x.shape, dtype=x.dtype) for x in args] + [pltpu.SemaphoreType.DMA((4,))],
        pltpu.HBM,
        56 * 2**20,
    )(*args)
    from_second = trade(second, "gy", 1)
    (from_second,) = local(hold, [(GROUP, depth * 8)])(from_second)
    from_first = trade(first, "gy", 0)
    packed = (-(-ROWS * (depth + 2) // 8) * 8, 128)
    near, far, closed = local(pack_rows, [packed, packed, (2, GROUP, depth * 8)])(
        field, first, second, from_second, from_first
    )
    (wide,) = local(widen, [(6, depth, 8, 256)], [scratch(depth * 8, 768)])(field, closed)
    far = trade(far, "gx", 1)
    near = lax.all_gather(near, "gx", axis_index_groups=[[i, i + 1] for i in range(0, rows, 2)])
    sent, basis, pots = local(
        moments,
        [(rows, 128), (3, 2, depth, 16, 256), (2, depth, 16, 256)],
        [scratch(1, depth, 16, 256), scratch(4, depth, 16, 256), scratch(2, depth, 16, 256), scratch(2, depth * 8, 768)],
    )(wide, near, far)
    received = lax.all_to_all(sent, "gx", 0, 0, tiled=True)
    (sent,) = local(relay, [(cols, 128)])(received)
    received = lax.all_to_all(sent, "gy", 0, 0, tiled=True)
    adjoint, gradient = local(
        finish,
        [cotangent.shape, conductance.shape],
        [scratch(2, depth, 16, 256)],
        kind=jax.ShapeDtypeStruct,
    )(received, basis, pots)
    return adjoint, gradient


def solution(mesh):
    return jax.shard_map(
        per_device,
        mesh=mesh,
        in_specs=(
            P(None, "gx", "gy"),
            P(None, "gx", "gy"),
            P(None, None, "gx", "gy"),
            P(None, None, "gx", "gy"),
        ),
        out_specs=(P(None, None, "gx", "gy"), P(None, "gx", "gy")),
        check_vma=False,
    )
```

```python
import jax
import jax.numpy as jnp
from jax import lax
from jax.experimental import pallas as pl
from jax.experimental.pallas import tpu as pltpu
from jax.sharding import PartitionSpec as P

SHIFT = 2.0
SPAN = 32.0
STEP_LOW = 1.0 / 61.0
SECOND = 64
COND, MASK, RES1, RES2, POT1, POT2 = range(6)
WIDTH = (3, 2, 3, 3, 1, 1)
LANE = (0, 9, 3, 6, 11, 12)
SLOT = (0, 6, 3, 8, 11, 12)
GROUP = 16
ROWS = sum(WIDTH)


def roll(x, amount, axis):
    amount = amount % x.shape[axis]
    return x if amount == 0 else pltpu.roll(x, amount, axis)


def fields_at(cond, labels, cot, saved, z):
    tag = labels[z]
    free = tag == 0
    mask = jnp.where(free, 1.0, 0.0)
    pots = [jnp.where(tag == k + 1, 1.0, jnp.where(free, saved[k, z], 0.0)) for k in range(2)]
    return [cond[z], mask] + [jnp.where(free, cot[k, z], 0.0) for k in range(2)] + pots


def lanes_of(shape=(8, 128)):
    return lax.broadcasted_iota(jnp.int32, shape, 1)


def within(index, low, count):
    return (index >= low) & (index < low + count)


def exact_dot(x, matrix):
    total = None
    for _ in range(3):
        term = x.astype(jnp.bfloat16)
        x = x - term.astype(jnp.float32)
        part = jnp.dot(term, matrix, preferred_element_type=jnp.float32)
        total = part if total is None else total + part
    return total


def difference_matrices():
    i = lax.broadcasted_iota(jnp.int32, (256, 256), 0)
    j = lax.broadcasted_iota(jnp.int32, (256, 256), 1)
    here = jnp.where(i == j, 1.0, 0.0)
    forward = here - jnp.where(i == (j + 1) % 256, 1.0, 0.0)
    backward = here - jnp.where((i + 1) % 256 == j, 1.0, 0.0)
    return forward.astype(jnp.bfloat16), backward.astype(jnp.bfloat16)


def place(shape, rows, cols, pairs):
    i = lax.broadcasted_iota(jnp.int32, shape, rows)
    j = lax.broadcasted_iota(jnp.int32, shape, cols)
    hit = i < 0
    for row, col, count in pairs:
        hit |= within(i, row, count) & (j - i == col - row)
    return jnp.where(hit, 1.0, 0.0).astype(jnp.bfloat16)


def pack_columns(cond_in, labels_in, cot_in, saved_in, first, second, field, cond, labels, cot, saved, sems):
    copies = [
        pltpu.make_async_copy(source, target, sems.at[i])
        for i, (source, target) in enumerate(
            ((cond_in, cond), (labels_in, labels), (cot_in, cot), (saved_in, saved))
        )
    ]
    for copy in copies:
        copy.start()
    picks = [
        place(
            (128, 128),
            0,
            1,
            [(0, LANE[f], WIDTH[f]), (128 - WIDTH[f], GROUP + LANE[f], WIDTH[f])],
        )
        for f in range(6)
    ]
    for copy in copies:
        copy.wait()
    even = lax.axis_index("gy") % 2 == 0
    depth = cond.shape[0]
    for z in range(depth):
        for f, x in enumerate(fields_at(cond, labels, cot, saved, z)):
            field[f, z] = x
    total = None
    for f in range(6):
        part = exact_dot(field[f].reshape(depth * 8, 128), picks[f])
        total = part if total is None else total + part
    columns = total.T
    left, right = columns[0:GROUP], columns[GROUP : 2 * GROUP]
    first[...] = jnp.where(even, right, left)
    second[...] = jnp.where(even, left, right)


def unpack_columns(left, right, out):
    packed = jnp.concatenate([left, right], axis=0).T
    for f in range(6):
        w = WIDTH[f]
        matrix = place(
            (2 * GROUP, 128), 0, 1, [(LANE[f], 128 - w, w), (GROUP + LANE[f], 0, w)]
        )
        out[:, f * 128 : (f + 1) * 128] = exact_dot(packed, matrix)


def hold(source, target):
    target[...] = source[...]


def pack_rows(field, sent_first, sent_second, from_second, from_first, near, far, closed):
    even = lax.axis_index("gy") % 2 == 0
    upper = lax.axis_index("gx") % 2 == 0
    depth = field.shape[1]
    slot = lax.broadcasted_iota(jnp.int32, (GROUP, 128), 0)
    c = LANE[COND]

    def choose(a, b):
        return jnp.where(even, a[...], b[...])

    left, right = choose(from_second, from_first), choose(from_first, from_second)
    own_left, own_right = choose(sent_second, sent_first), choose(sent_first, sent_second)
    pot = (slot == LANE[POT1]) | (slot == LANE[POT2])
    outside = right[c : c + 1] == 0.0
    right = jnp.where(outside & (slot == c), -roll(own_right, -2, 0), right)
    right = jnp.where(outside & pot, own_right, right)
    outside = left[c + 2 : c + 3] == 0.0
    left = jnp.where(outside & (slot == c + 2), -roll(own_left, 2, 0), left)
    left = jnp.where(outside & pot, own_left, left)
    columns = jnp.concatenate([left[0:ROWS], right[0:ROWS]], axis=0)
    start, end = ROWS * depth, ROWS * (depth + 2)
    for out in (near, far):
        out[start:end] = columns
        if out.shape[0] > end:
            out[end:] = jnp.zeros((out.shape[0] - end, 128), jnp.float32)
    closed[0] = left
    closed[1] = right
    for z in range(depth):
        fields = [field[f, z] for f in range(6)]
        own = []
        for side in range(2):
            rows = []
            for f in (COND, RES1, MASK, RES2, POT1, POT2):
                w = WIDTH[f]
                start = 0 if side == 0 else 8 - w
                rows.append(fields[f][start : start + w])
            own.append(jnp.concatenate(rows, axis=0))
        near[ROWS * z : ROWS * (z + 1)] = jnp.where(upper, own[1], own[0])
        far[ROWS * z : ROWS * (z + 1)] = jnp.where(upper, own[0], own[1])


def widen(field, closed, wide, halo):
    unpack_columns(closed[0], closed[1], halo)
    for z in range(field.shape[1]):
        for f in range(6):
            wide[f, z, :, 0:128] = field[f, z]
            wide[f, z, :, 128:256] = halo[8 * z : 8 * z + 8, f * 128 : (f + 1) * 128]


def moments(wide, from_near, from_far, sent, basis, pots, field, weight, flux, corner):
    depth = wide.shape[1]
    core = lax.axis_index("gx") % 2
    lane16 = lanes_of((16, 128))
    row8 = lax.broadcasted_iota(jnp.int32, (8, 256), 0)

    def above(i):
        rows = slice(ROWS * i, ROWS * (i + 1))
        return jnp.where(core == 0, from_far[rows], from_near[1 - core, rows])

    def below(i):
        rows = slice(ROWS * i, ROWS * (i + 1))
        return jnp.where(core == 0, from_near[1 - core, rows], from_far[rows])

    blank = jnp.zeros((GROUP - ROWS, 128), jnp.float32)
    for side, source in enumerate((above, below)):
        tips = [jnp.concatenate([source(depth + i), blank], axis=0) for i in range(2)]
        unpack_columns(*tips, corner.at[side])
    for z in range(depth):
        top, bottom = above(z), below(z)
        parts = []
        for f in range(6):
            w, s = WIDTH[f], SLOT[f]
            own = wide[f, z]
            gap = jnp.zeros((8 - 2 * w, 128), jnp.float32)
            low = jnp.concatenate([bottom[s : s + w], gap, top[s : s + w]], axis=0)
            tips = [
                corner[side, 8 * z : 8 * z + 8, f * 128 : (f + 1) * 128] for side in range(2)
            ]
            high = jnp.concatenate([tips[1][0:w], gap, tips[0][8 - w : 8]], axis=0)
            parts.append((own, jnp.concatenate([low, high], axis=1)))
        own, other = parts[COND]
        outside = (other == 0.0) & ((row8 == 0) | (row8 == 7))

        def edge_value(x):
            return jnp.where(row8 == 0, roll(x, 1, 0), roll(x, -1, 0))

        parts[COND] = (own, jnp.where(outside, -edge_value(own), other))
        for f in (POT1, POT2):
            own, other = parts[f]
            parts[f] = (own, jnp.where(outside, edge_value(own), other))
        field[0, z, 0:8], field[0, z, 8:16] = parts[COND]
        weight[3, z, 0:8] = parts[MASK][0] * (1.0 / SPAN)
        weight[3, z, 8:16] = parts[MASK][1] * (1.0 / SPAN)
        for k in range(2):
            basis[0, k, z, 0:8], basis[0, k, z, 8:16] = parts[RES1 + k]
            pots[k, z, 0:8], pots[k, z, 8:16] = parts[POT1 + k]
    for z in range(depth):
        c = field[0, z]
        weight[0, z] = 0.5 * (c + roll(c, -1, 0))
        weight[1, z] = 0.5 * (c + roll(c, -1, 1))
        if z + 1 < depth:
            weight[2, z] = 0.5 * (c + field[0, z + 1])

    forward, backward = difference_matrices()

    def image(k, z, source, carry):
        u = basis[source, k, z]
        fx = weight[0, z] * (u - roll(u, -1, 0))
        total = (fx - roll(fx, 1, 0)) + flux[k, z] - u
        if carry is not None:
            total = total - carry
        carry = None
        if z + 1 < depth:
            carry = weight[2, z] * (u - basis[source, k, z + 1])
            total = total + carry
        return weight[3, z] * total, carry

    def lane_fluxes(source, rows):
        for k in range(2):
            u = basis[source, k, :, 0:rows].reshape(depth * rows, 256)
            f = weight[1, :, 0:rows].reshape(depth * rows, 256) * exact_dot(u, forward)
            flux[k, :, 0:rows] = exact_dot(f, backward).reshape(depth, rows, 256)

    for power in range(2):
        lane_fluxes(power, 16)
        for k in range(2):
            carry = None
            for z in range(depth):
                value, carry = image(k, z, power, carry)
                basis[power + 1, k, z] = value
    own = (slice(0, 8), slice(0, 128))

    def own_image(k, z, carry):
        u = basis[2, k, z, :, 0:128]
        fx = weight[0, z, :, 0:128] * (u - roll(u, -1, 0))
        u = u[0:8]
        total = (fx - roll(fx, 1, 0))[0:8] + flux[k, z, 0:8, 0:128] - u
        if carry is not None:
            total = total - carry
        carry = None
        if z + 1 < depth:
            carry = weight[2, z, 0:8, 0:128] * (u - basis[2, k, z + 1, 0:8, 0:128])
            total = total + carry
        return weight[3, z, 0:8, 0:128] * total, carry

    lane_fluxes(2, 8)
    totals = []
    for k in range(2):
        sums = [jnp.zeros((8, 128), jnp.float32) for _ in range(6)]
        carry = None
        for z in range(depth):
            last, carry = own_image(k, z, carry)
            v = [basis[i, k, z, 0:8, 0:128] for i in range(3)] + [last]
            sums = [s + v[i // 2] * v[i - i // 2] for i, s in enumerate(sums)]
        totals += sums
    sub = lax.broadcasted_iota(jnp.int32, (16, 128), 0)
    packed = jnp.zeros((16, 128), jnp.float32)
    for i, s in enumerate(totals):
        packed = jnp.where(sub == i, jnp.sum(s, axis=0, keepdims=True), packed)
    packed = jnp.sum(packed, axis=1, keepdims=True)
    target = jnp.where(sub < 6, sub, sub - 6 + SECOND)
    row = jnp.sum(jnp.where((lane16 == target) & (sub < 12), packed, 0.0), axis=0, keepdims=True)
    sent[...] = jnp.broadcast_to(row, sent.shape)


def relay(received, sent):
    sent[...] = jnp.broadcast_to(jnp.sum(received[...], axis=0, keepdims=True), sent.shape)


def coefficients(nu):
    def inner(a, b, lift):
        total = None
        for i, x in enumerate(a):
            for j, y in enumerate(b):
                term = (x * y) * nu[i + j + lift]
                total = term if total is None else total + term
        return total

    residual = [jnp.ones_like(nu[0])]
    direction = residual
    answer = []
    norm = nu[0]
    for iteration in range(3):
        energy = SHIFT * inner(direction, direction, 0) + SPAN * inner(direction, direction, 1)
        step = jnp.clip(norm / energy, STEP_LOW, 1.0)
        answer = [a + step * d for a, d in zip(answer + [0.0], direction)]
        if iteration == 2:
            return answer
        image = [SHIFT * d for d in direction] + [0.0]
        image = [i + SPAN * d for i, d in zip(image, [0.0] + direction)]
        residual = [r - step * i for r, i in zip(residual + [0.0], image)]
        new = jnp.maximum(inner(residual, residual, 0), 0.0)
        ratio = new / norm
        direction = [r + ratio * d for r, d in zip(residual, direction + [0.0])]
        norm = new


def finish(received, basis, pots, adjoint, gradient, field):
    depth = basis.shape[2]
    row = jnp.sum(received[...], axis=0, keepdims=True)
    row = jnp.broadcast_to(row, (8, 128))
    combined = coefficients([roll(row, -i, 1) for i in range(6)])
    lane = lanes_of()
    scale = [
        [
            jnp.sum(jnp.where(lane == k * SECOND, c, 0.0), axis=1, keepdims=True)[0:1, 0:1]
            for c in combined
        ]
        for k in range(2)
    ]
    for k in range(2):
        c = [jnp.broadcast_to(x, (16, 256)) for x in scale[k]]
        for z in range(depth):
            value = c[0] * basis[0, k, z] + c[1] * basis[1, k, z] + c[2] * basis[2, k, z]
            field[k, z] = value
            adjoint[k, z] = value[0:8, 0:128]
    carry = None
    for z in range(depth):
        gx = gy = gz = None
        for k in range(2):
            a, p = field[k, z], pots[k, z]
            ty = (a[0:8] - roll(a[0:8], -1, 1)) * (p[0:8] - roll(p[0:8], -1, 1))
            a, p = a[:, 0:128], p[:, 0:128]
            tx = (a - roll(a, -1, 0)) * (p - roll(p, -1, 0))
            gx = tx if gx is None else gx + tx
            gy = ty if gy is None else gy + ty
            if z + 1 < depth:
                tz = (a[0:8] - field[k, z + 1, 0:8, 0:128]) * (
                    p[0:8] - pots[k, z + 1, 0:8, 0:128]
                )
                gz = tz if gz is None else gz + tz
        total = (gx + roll(gx, 1, 0))[0:8] + (gy + roll(gy, 1, 1))[:, 0:128]
        if carry is not None:
            total = total + carry
        if gz is not None:
            total = total + gz
        carry = gz
        gradient[z] = -0.5 * total


def local(body, outs, scratch=(), space=pltpu.VMEM, limit=32 * 2**20, kind=pltpu.VMEM):
    vmem = pl.BlockSpec(memory_space=pltpu.VMEM)
    shapes = [kind(s, jnp.float32) for s in outs]

    def call(*args):
        return pl.pallas_call(
            body,
            out_shape=shapes,
            in_specs=[pl.BlockSpec(memory_space=space)] * len(args),
            out_specs=[vmem] * len(outs),
            scratch_shapes=list(scratch),
            compiler_params=pltpu.CompilerParams(vmem_limit_bytes=limit),
        )(*args)

    return call


def scratch(*shape, dtype=jnp.float32):
    return pltpu.VMEM(shape, dtype)


def trade(x, axis, start):
    pairs = [(i, i + 1) for i in range(start, lax.axis_size(axis) - 1, 2)]
    return lax.ppermute(x, axis, pairs + [(j, i) for i, j in pairs])


def per_device(conductance, labels, cotangent, saved):
    depth = conductance.shape[0]
    rows, cols = lax.axis_size("gx"), lax.axis_size("gy")
    args = (conductance, labels, cotangent, saved)
    first, second, field = local(
        pack_columns,
        [(GROUP, depth * 8)] * 2 + [(6, depth, 8, 128)],
        [scratch(*x.shape, dtype=x.dtype) for x in args] + [pltpu.SemaphoreType.DMA((4,))],
        pltpu.HBM,
        56 * 2**20,
    )(*args)
    from_second = trade(second, "gy", 1)
    (from_second,) = local(hold, [(GROUP, depth * 8)])(from_second)
    from_first = trade(first, "gy", 0)
    packed = (-(-ROWS * (depth + 2) // 8) * 8, 128)
    near, far, closed = local(pack_rows, [packed, packed, (2, GROUP, depth * 8)])(
        field, first, second, from_second, from_first
    )
    (wide,) = local(widen, [(6, depth, 8, 256)], [scratch(depth * 8, 768)])(field, closed)
    far = trade(far, "gx", 1)
    near = lax.all_gather(near, "gx", axis_index_groups=[[i, i + 1] for i in range(0, rows, 2)])
    sent, basis, pots = local(
        moments,
        [(rows, 128), (3, 2, depth, 16, 256), (2, depth, 16, 256)],
        [scratch(1, depth, 16, 256), scratch(4, depth, 16, 256), scratch(2, depth, 16, 256), scratch(2, depth * 8, 768)],
    )(wide, near, far)
    received = lax.all_to_all(sent, "gx", 0, 0, tiled=True)
    (sent,) = local(relay, [(cols, 128)])(received)
    received = lax.all_to_all(sent, "gy", 0, 0, tiled=True)
    adjoint, gradient = local(
        finish,
        [cotangent.shape, conductance.shape],
        [scratch(2, depth, 16, 256)],
        kind=jax.ShapeDtypeStruct,
    )(received, basis, pots)
    return adjoint, gradient


def solution(mesh):
    return jax.shard_map(
        per_device,
        mesh=mesh,
        in_specs=(
            P(None, "gx", "gy"),
            P(None, "gx", "gy"),
            P(None, None, "gx", "gy"),
            P(None, None, "gx", "gy"),
        ),
        out_specs=(P(None, None, "gx", "gy"), P(None, "gx", "gy")),
        check_vma=False,
    )
```
